32 devices in a mesh: groups: 2 (over x), chan: 16 (over z, y, core).
Axes of the slice: x: 2, y: 2, z: 4, core: 2. Of those that a mesh axis runs over, the one named last changes fastest.
Arguments:
- samples: bfloat16 [2048, 2, 143, 256], P(('groups', 'chan')), parts along dimension 0, may hold values from -6 to 6
- flags: int32 [2048], P('groups'), parts along dimension 0, may hold values 0 or 1
- delays: int32 [256, 1024], replicated, may hold values from 0 to 255
- order: int32 [2048], P('groups'), parts along dimension 0, may hold values from 0 to 1023, each once
Outputs:
- visibilities: bfloat16 [512, 36, 2, 128, 128], P(('groups', 'chan')), parts along dimension 0
- beam_voltages: bfloat16 [512, 2, 113, 256], P(('groups', 'chan')), parts along dimension 0
The draws below stay inside these ranges and needn't reach their ends.
There are 2 independent parts, one for each index of `groups`. The reference program is written for one: setup_inputs(seed, part) draws one part's arguments, and reference() takes and returns one part's arrays. A program takes and returns all parts, laid end to end along the dimension named above; an argument that names none is the same for every part. Nothing has to cross between parts.
Inputs may be any that keep to these rules, and one draw needn't show every extreme that they name: `order`: each antenna appears once.
All inputs are finite; a program needn't handle non-finite values.
Results may differ from the reference program's by a relative error of at most 0.008.
Values may be sent and summed in bfloat16 or wider, within the bound.
No kernel may reach another device: no remote copies, remote signals or barrier semaphores. Data moves between devices by JAX's collectives and lax.ppermute only.
A program may use at most 128 MiB of HBM per device.

```python
import math
import jax
import jax.numpy as jnp
import numpy as np
from jax import lax

ANTENNA_INPUTS = 1024
CHANNEL_COUNT = 256
VOLTAGE_BEAMS = 256
TAPS = 16
TILE_ANTENNAS = 128
WINDOW_SPECTRA = 128
INPUT_FRAMES = 143
OUTFRAMES = 113


def set_ends(result, rng, low, largest):
    shape = result.shape
    spot = [jax.random.randint(jax.random.fold_in(rng, axis), (), 0, shape[axis]) for axis in range(len(shape))]
    result = result.at[tuple(spot)].set(low)
    longest = shape.index(max(shape))
    spot[longest] = (spot[longest] + 1) % shape[longest]
    return result.at[tuple(spot)].set(largest)


def steps_of(rng, shape, cuts, least, largest):
    loudness, own = 1.0, jax.random.fold_in(rng, 6)
    for axis_at, parts in cuts:
        steps = jnp.exp(jax.random.uniform(jax.random.fold_in(own, axis_at), (parts,), jnp.float32, least / len(cuts), largest / len(cuts)))
        loudness = loudness * jnp.repeat(steps, shape[axis_at] // parts).reshape([-1 if axis == axis_at else 1 for axis in range(len(shape))])
    return loudness


def normal_values(stream_key, extent, deviation, most, shards=(), kind=jnp.bfloat16):
    level = steps_of(stream_key, extent, shards, -0.22, 0.18) if shards else 1.0
    result = jax.random.normal(stream_key, extent, jnp.float32) * deviation * level
    return jnp.minimum(jnp.maximum(result, -most), most).astype(kind)


def setup_inputs(seed: int = 0, part: int = 0) -> dict:
    streams_of = jax.random.split(jax.random.key(seed), 5)
    own_keys = jax.random.split(jax.random.fold_in(streams_of[4], part), 5)
    return {
        "samples": normal_values(own_keys[0], (ANTENNA_INPUTS, 2, INPUT_FRAMES, CHANNEL_COUNT), 1.0, 6.0, ((0, 16),)),
        "flags": set_ends((jax.random.randint(own_keys[1], (ANTENNA_INPUTS,), 0, 8) < 7).astype(jnp.int32), jax.random.fold_in(own_keys[1], 1), 0, 1),
        "delays": set_ends(jax.random.randint(streams_of[2], (VOLTAGE_BEAMS, ANTENNA_INPUTS), 0, CHANNEL_COUNT), jax.random.fold_in(streams_of[2], 1), 0, CHANNEL_COUNT - 1).astype(jnp.int32),
        "order": jax.random.permutation(own_keys[3], ANTENNA_INPUTS).astype(jnp.int32),
    }


def prototype():
    length = TAPS * CHANNEL_COUNT
    counter = jnp.arange(length, dtype=jnp.float32)
    shifted = (counter - (length - 1) / 2.0) / CHANNEL_COUNT
    window = 0.5 - 0.5 * jnp.cos(2.0 * math.pi * (counter + 0.5) / length)
    return (jnp.sinc(shifted) * window).reshape(TAPS, CHANNEL_COUNT)

def dft_table(direction):
    counter = jnp.arange(CHANNEL_COUNT, dtype=jnp.int32)
    phase = counter[:, None] * counter[None, :] % CHANNEL_COUNT
    angle = phase.astype(jnp.float32) * (2.0 * math.pi / CHANNEL_COUNT)
    cosine = jnp.cos(angle)
    sine = jnp.sin(angle)
    top_rows = jnp.stack([cosine, -direction * sine], axis=1)
    bottom_rows = jnp.stack([direction * sine, cosine], axis=1)
    return jnp.stack([top_rows, bottom_rows], axis=0).astype(jnp.bfloat16)

def tile_pairs(tile_count):
    first_tiles = []
    second_tiles = []
    for row_tile in range(tile_count):
        for col_tile in range(row_tile, tile_count):
            first_tiles.append(row_tile)
            second_tiles.append(col_tile)
    return (np.array(first_tiles, np.int32), np.array(second_tiles, np.int32))

def reference(samples, flags, delays, order):
    filt = prototype()
    filtered_frames = jnp.zeros((ANTENNA_INPUTS, 2, WINDOW_SPECTRA, CHANNEL_COUNT), jnp.float32)
    for tap_step in range(TAPS):
        filtered_frames = filtered_frames + filt[tap_step] * samples[:, :, tap_step:tap_step + WINDOW_SPECTRA, :].astype(jnp.float32)
    filtered_frames = filtered_frames.astype(jnp.bfloat16)
    forward = dft_table(1.0)
    channel_spectra = jnp.einsum('arsj,rjuk->kaus', filtered_frames.astype(jnp.float32), forward.astype(jnp.float32))
    channel_spectra = (channel_spectra * (1.0 / math.sqrt(CHANNEL_COUNT))).astype(jnp.bfloat16).reshape(CHANNEL_COUNT, ANTENNA_INPUTS, 2 * WINDOW_SPECTRA)
    flag_values = flags.astype(jnp.bfloat16)
    masked = channel_spectra * flag_values[None, :, None]
    permuted = jnp.take(masked, order, axis=1)
    tile_count = ANTENNA_INPUTS // TILE_ANTENNAS
    first_tiles, second_tiles = tile_pairs(tile_count)

    def correlate(channel_rows):
        other = jnp.concatenate([channel_rows[:, WINDOW_SPECTRA:], -channel_rows[:, :WINDOW_SPECTRA]], axis=1)
        stacked = jnp.stack([channel_rows, other], axis=0).reshape(2, tile_count, TILE_ANTENNAS, 2 * WINDOW_SPECTRA)
        picked = stacked[:, first_tiles]
        columns = channel_rows.reshape(tile_count, TILE_ANTENNAS, 2 * WINDOW_SPECTRA)[second_tiles]
        product = jnp.einsum('upis,pjs->puij', picked.astype(jnp.float32), columns.astype(jnp.float32))
        return (product * (1.0 / WINDOW_SPECTRA)).astype(jnp.bfloat16)
    visibilities = lax.map(correlate, permuted)

    def beamform(packed):
        channel_rows, channel = packed
        phase = delays * channel % CHANNEL_COUNT
        angle = phase.astype(jnp.float32) * (2.0 * math.pi / CHANNEL_COUNT)
        weights = jnp.concatenate([jnp.cos(angle), jnp.sin(angle)], axis=1).astype(jnp.bfloat16)
        other = jnp.concatenate([channel_rows[:, WINDOW_SPECTRA:], -channel_rows[:, :WINDOW_SPECTRA]], axis=1)
        stacked = jnp.concatenate([channel_rows, other], axis=0)
        formed_beams = jnp.dot(weights, stacked, preferred_element_type=jnp.float32)
        return (formed_beams * (1.0 / math.sqrt(ANTENNA_INPUTS))).astype(jnp.bfloat16)
    beams = lax.map(beamform, (masked, jnp.arange(CHANNEL_COUNT, dtype=jnp.int32)))
    arranged = beams.transpose(1, 0, 2).reshape(VOLTAGE_BEAMS, CHANNEL_COUNT, 2, WINDOW_SPECTRA)
    inverse = dft_table(-1.0)
    zeta = jnp.einsum('bkrs,rkuj->busj', arranged.astype(jnp.float32), inverse.astype(jnp.float32))
    zeta = (zeta * (1.0 / math.sqrt(CHANNEL_COUNT))).astype(jnp.bfloat16)
    output = jnp.zeros((VOLTAGE_BEAMS, 2, OUTFRAMES, CHANNEL_COUNT), jnp.float32)
    for tap_step in range(TAPS):
        output = output + filt[TAPS - 1 - tap_step] * zeta[:, :, tap_step:tap_step + OUTFRAMES, :].astype(jnp.float32)
    return (visibilities, output.astype(jnp.bfloat16))
```

```python
import functools
import math

import jax
import jax.numpy as jnp
import ml_dtypes
import numpy as np
from jax import lax
from jax.experimental import pallas as pl
from jax.experimental.pallas import tpu as pltpu
from jax.sharding import PartitionSpec as P

TAPS = 16
TILE_ANTENNAS = 128
BLOCK_ANTENNAS = 16
LANES = 128
VMEM_BYTES = 60 * 1024 * 1024


def prototype(tap_count, chan_count):
    length = tap_count * chan_count
    counter = np.arange(length, dtype=np.float32)
    shifted = (counter - np.float32((length - 1) / 2.0)) / np.float32(chan_count)
    window = 0.5 - 0.5 * np.cos(2.0 * math.pi * (counter + 0.5) / length)
    return (np.sinc(shifted) * window).astype(np.float32).reshape(tap_count, chan_count)


def dft_parts(chan_count):
    counter = np.arange(chan_count)
    angle = (counter[:, None] * counter[None, :] % chan_count) * (2.0 * math.pi / chan_count)
    return np.cos(angle), np.sin(angle)


def round_bf16(table):
    return table.astype(np.float32).astype(ml_dtypes.bfloat16)


def forward_table(chan_count):
    cosine, sine = dft_parts(chan_count)
    table = np.concatenate(
        [np.concatenate([cosine, sine], axis=1), np.concatenate([-sine, cosine], axis=1)], axis=0
    )
    return (round_bf16(table).astype(np.float32) / math.sqrt(chan_count)).astype(
        ml_dtypes.bfloat16
    )


def inverse_table(chan_count):
    cosine, sine = dft_parts(chan_count)
    table = np.concatenate(
        [np.concatenate([cosine, sine], axis=1), np.concatenate([-sine, cosine], axis=1)], axis=0
    )
    return (round_bf16(table).astype(np.float32) / math.sqrt(chan_count)).astype(
        ml_dtypes.bfloat16
    )


def channelize_kernel(samples_ref, proto_ref, table_ref, out_ref, frames, filtered, turned):
    block, _, in_frames, chans = samples_ref.shape
    spectra = turned.shape[2]

    def pair(step, carry):
        for half in range(2):
            ant = 2 * step + half
            for part in range(2):
                for lane in range(0, chans, LANES):
                    cols = slice(lane, lane + LANES)
                    frames[0:in_frames, :] = samples_ref[ant, part, :, cols].astype(jnp.float32)
                    total = proto_ref[0:1, cols] * frames[pl.ds(0, spectra), :]
                    for tap in range(1, TAPS):
                        total = total + proto_ref[tap : tap + 1, cols] * frames[pl.ds(tap, spectra), :]
                    filtered[
                        half * spectra : (half + 1) * spectra,
                        part * chans + lane : part * chans + lane + LANES,
                    ] = total.astype(jnp.bfloat16)
        product = lax.dot_general(
            table_ref[...],
            filtered[...],
            (((1,), (1,)), ((), ())),
            preferred_element_type=jnp.float32,
        )
        for half in range(2):
            for part in range(2):
                turned[part, pl.ds(2 * step + half, chans, stride=block), :] = product[
                    part * chans : (part + 1) * chans, half * spectra : (half + 1) * spectra
                ]
        return carry

    lax.fori_loop(0, block // 2, pair, 0)
    for part in range(2):
        out_ref[:, :, part * spectra : (part + 1) * spectra] = (
            turned[part].reshape(chans, block, spectra).astype(jnp.bfloat16)
        )


def channelize(samples, proto, table, first, count, block):
    _, _, in_frames, chans = samples.shape
    spectra = in_frames - TAPS + 1

    return pl.pallas_call(
        channelize_kernel,
        grid=(count // block,),
        in_specs=[
            pl.BlockSpec((block, 2, in_frames, chans), lambda i: (i + first // block, 0, 0, 0)),
            pl.BlockSpec((TAPS, chans), lambda i: (0, 0)),
            pl.BlockSpec((2 * chans, 2 * chans), lambda i: (0, 0)),
        ],
        out_specs=pl.BlockSpec((chans, block, 2 * spectra), lambda i: (0, i, 0)),
        out_shape=jax.ShapeDtypeStruct((chans, count, 2 * spectra), jnp.bfloat16),
        scratch_shapes=[
            pltpu.VMEM((in_frames + 1, LANES), jnp.float32),
            pltpu.VMEM((2 * spectra, 2 * chans), jnp.bfloat16),
            pltpu.VMEM((2, chans * block, spectra), jnp.float32),
        ],
        compiler_params=pltpu.CompilerParams(vmem_limit_bytes=VMEM_BYTES),
        cost_estimate=pl.CostEstimate(
            flops=count * spectra * 4 * chans * 2 * chans * 2,
            bytes_accessed=count * 2 * (in_frames + spectra) * chans * 2,
            transcendentals=0,
        ),
        name="channelize",
    )(samples, proto, table)


def beam_kernel(counts, *refs):
    x_refs = refs[: len(counts)]
    weights_ref, out_ref, turned = refs[len(counts) :]
    channel = pl.program_id(0)
    beams = out_ref.shape[0]
    local = out_ref.shape[1]
    spectra = turned.shape[2]
    product = None
    start = 0
    for x_ref, count in zip(x_refs, counts):
        rows = x_ref[:, 0].reshape(count, 2 * spectra)
        term = jnp.dot(
            weights_ref[0, :, start : start + count], rows, preferred_element_type=jnp.float32
        )
        product = term if product is None else product + term
        start += count
    turned[0, pl.ds(channel, beams, stride=local), :] = (
        product[:beams, :spectra] + product[beams:, spectra:]
    )
    turned[1, pl.ds(channel, beams, stride=local), :] = (
        product[:beams, spectra:] - product[beams:, :spectra]
    )

    @pl.when(channel == pl.num_programs(0) - 1)
    def _():
        for part in range(2):
            out_ref[:, :, part * spectra : (part + 1) * spectra] = (
                turned[part].reshape(beams, local, spectra).astype(jnp.bfloat16)
            )


def form_beams(blocks, weights):
    local, double_beams, antennas = weights.shape
    beams = double_beams // 2
    columns = blocks[0].shape[3]
    counts = tuple(x.shape[0] * x.shape[2] for x in blocks)
    return pl.pallas_call(
        functools.partial(beam_kernel, counts),
        grid=(local,),
        in_specs=[
            pl.BlockSpec((x.shape[0], 1, x.shape[2], columns), lambda c: (0, c, 0, 0))
            for x in blocks
        ]
        + [pl.BlockSpec((1, double_beams, antennas), lambda c: (c, 0, 0))],
        out_specs=pl.BlockSpec((beams, local, columns), lambda c: (0, 0, 0)),
        out_shape=jax.ShapeDtypeStruct((beams, local, columns), jnp.bfloat16),
        scratch_shapes=[pltpu.VMEM((2, beams * local, columns // 2), jnp.float32)],
        compiler_params=pltpu.CompilerParams(vmem_limit_bytes=VMEM_BYTES),
        cost_estimate=pl.CostEstimate(
            flops=2 * local * double_beams * antennas * columns,
            bytes_accessed=2 * local * (double_beams * antennas + antennas * columns + beams * columns),
            transcendentals=0,
        ),
        name="form_beams",
    )(*blocks, weights)


def visibility_kernel(counts, order_ref, ids_ref, flags_ref, *refs):
    x_refs = refs[: len(counts)]
    out_ref, select, permuted, turned = refs[len(counts) :]
    antennas, columns = permuted.shape
    spectra = columns // 2
    tile = TILE_ANTENNAS
    tiles = antennas // tile

    @pl.when(pl.program_id(0) == 0)
    def _():
        for t in range(tiles):
            rows = slice(t * tile, (t + 1) * tile)
            select[rows, :] = jnp.where(
                order_ref[rows, :] == ids_ref[...], flags_ref[...], 0.0
            ).astype(jnp.bfloat16)

    product = None
    start = 0
    for x_ref, count in zip(x_refs, counts):
        term = jnp.dot(
            select[:, start : start + count],
            x_ref[:, 0].reshape(count, columns),
            preferred_element_type=jnp.float32,
        )
        product = term if product is None else product + term
        start += count
    permuted[...] = product.astype(jnp.bfloat16)
    scaled = product * (1.0 / spectra)
    for t in range(tiles):
        block = scaled[t * tile : (t + 1) * tile, :]
        turned[2 * t * tile : (2 * t + 1) * tile, :] = block.astype(jnp.bfloat16)
        turned[(2 * t + 1) * tile : (2 * t + 2) * tile, :spectra] = block[:, spectra:].astype(jnp.bfloat16)
        turned[(2 * t + 1) * tile : (2 * t + 2) * tile, spectra:] = (-block[:, :spectra]).astype(jnp.bfloat16)
    pair = 0
    for p in range(tiles):
        left = turned[2 * p * tile : (2 * p + 2) * tile, :]
        result = lax.dot_general(
            left,
            permuted[p * tile :, :],
            (((1,), (1,)), ((), ())),
            preferred_element_type=jnp.float32,
        ).astype(jnp.bfloat16)
        for q in range(p, tiles):
            cols = slice((q - p) * tile, (q - p + 1) * tile)
            out_ref[0, pair, 0] = result[:tile, cols]
            out_ref[0, pair, 1] = result[tile:, cols]
            pair += 1


def correlate(blocks, order, ids, flags):
    antennas = order.shape[0]
    local, columns = blocks[0].shape[1], blocks[0].shape[3]
    counts = tuple(x.shape[0] * x.shape[2] for x in blocks)
    tiles = antennas // TILE_ANTENNAS
    pairs = tiles * (tiles + 1) // 2
    return pl.pallas_call(
        functools.partial(visibility_kernel, counts),
        grid=(local,),
        in_specs=[
            pl.BlockSpec((antennas, 1), lambda c: (0, 0)),
            pl.BlockSpec((1, antennas), lambda c: (0, 0)),
            pl.BlockSpec((1, antennas), lambda c: (0, 0)),
        ]
        + [
            pl.BlockSpec((x.shape[0], 1, x.shape[2], columns), lambda c: (0, c, 0, 0))
            for x in blocks
        ],
        out_specs=pl.BlockSpec(
            (1, pairs, 2, TILE_ANTENNAS, TILE_ANTENNAS), lambda c: (c, 0, 0, 0, 0)
        ),
        out_shape=jax.ShapeDtypeStruct(
            (local, pairs, 2, TILE_ANTENNAS, TILE_ANTENNAS), jnp.bfloat16
        ),
        scratch_shapes=[
            pltpu.VMEM((antennas, antennas), jnp.bfloat16),
            pltpu.VMEM((antennas, columns), jnp.bfloat16),
            pltpu.VMEM((2 * antennas, columns), jnp.bfloat16),
        ],
        compiler_params=pltpu.CompilerParams(vmem_limit_bytes=VMEM_BYTES),
        cost_estimate=pl.CostEstimate(
            flops=2 * local * columns * (antennas * antennas + pairs * 2 * TILE_ANTENNAS**2),
            bytes_accessed=2 * local * (antennas * columns + pairs * 2 * TILE_ANTENNAS**2),
            transcendentals=0,
        ),
        name="correlate",
    )(order[:, None], ids[None, :], flags[None, :], *blocks)


def synthesize_kernel(beams_ref, proto_ref, table_ref, out_ref, zeta):
    sources, _, local, columns = beams_ref.shape
    chans = sources * local
    spectra = columns // 2
    out_frames = out_ref.shape[2]
    rows = beams_ref[:, 0].reshape(chans, columns)
    for part in range(2):
        cols = slice(part * chans, (part + 1) * chans)
        value = None
        for source in range(2):
            term = lax.dot_general(
                rows[:, source * spectra : (source + 1) * spectra],
                table_ref[source * chans : (source + 1) * chans, cols],
                (((0,), (0,)), ((), ())),
                preferred_element_type=jnp.float32,
            )
            value = term if value is None else value + term
        value = value.astype(jnp.bfloat16).astype(jnp.float32)
        for lane in range(0, chans, LANES):
            zeta[...] = value[:, lane : lane + LANES]
            total = proto_ref[TAPS - 1 : TAPS, lane : lane + LANES] * zeta[pl.ds(0, out_frames), :]
            for tap in range(1, TAPS):
                total = total + (
                    proto_ref[TAPS - 1 - tap : TAPS - tap, lane : lane + LANES]
                    * zeta[pl.ds(tap, out_frames), :]
                )
            out_ref[0, part, :, lane : lane + LANES] = total.astype(jnp.bfloat16)


def synthesize(arranged, proto, table):
    sources, beams, local, columns = arranged.shape
    chans = sources * local
    spectra = columns // 2
    out_frames = spectra - TAPS + 1
    return pl.pallas_call(
        synthesize_kernel,
        grid=(beams,),
        in_specs=[
            pl.BlockSpec((sources, 1, local, columns), lambda b: (0, b, 0, 0)),
            pl.BlockSpec((TAPS, chans), lambda b: (0, 0)),
            pl.BlockSpec((2 * chans, 2 * chans), lambda b: (0, 0)),
        ],
        out_specs=pl.BlockSpec((1, 2, out_frames, chans), lambda b: (b, 0, 0, 0)),
        out_shape=jax.ShapeDtypeStruct((beams, 2, out_frames, chans), jnp.bfloat16),
        scratch_shapes=[pltpu.VMEM((spectra, LANES), jnp.float32)],
        compiler_params=pltpu.CompilerParams(vmem_limit_bytes=VMEM_BYTES),
        cost_estimate=pl.CostEstimate(
            flops=2 * beams * spectra * 4 * chans * chans,
            bytes_accessed=2 * beams * (columns + 2 * out_frames) * chans,
            transcendentals=0,
        ),
        name="synthesize",
    )(arranged, proto, table)


def per_device(samples, flags, delays, order):
    devices = lax.axis_size("chan")
    antennas_here, _, in_frames, chans = samples.shape
    local_channels = chans // devices
    spectra = in_frames - TAPS + 1
    antennas = antennas_here * devices
    beam_count = delays.shape[0]
    block = BLOCK_ANTENNAS if antennas_here % BLOCK_ANTENNAS == 0 else antennas_here
    sizes = [block, antennas_here - block] if antennas_here > block else [block]

    proto = jnp.asarray(prototype(TAPS, chans))
    forward = jnp.asarray(forward_table(chans))
    inverse = jnp.asarray(inverse_table(chans))

    blocks = []
    columns_of = []
    start = 0
    for size in sizes:
        part = channelize(samples, proto, forward, start, size, block)
        part = lax.all_to_all(part, "chan", split_axis=0, concat_axis=0, tiled=True)
        blocks.append(part.reshape(devices, local_channels, size, 2 * spectra))
        ids = np.arange(antennas, dtype=np.int32).reshape(devices, antennas_here)
        columns_of.append(ids[:, start : start + size].reshape(-1))
        start += size
    ids = np.concatenate(columns_of)

    def arrange(x):
        x = x.reshape(x.shape[:-1] + (devices, antennas_here))
        pieces = []
        at = 0
        for size in sizes:
            pieces.append(x[..., at : at + size].reshape(x.shape[:-2] + (devices * size,)))
            at += size
        return jnp.concatenate(pieces, axis=-1)

    flag_row = arrange(flags).astype(jnp.float32)
    channel_ids = lax.axis_index("chan") * local_channels + jnp.arange(
        local_channels, dtype=jnp.int32
    )
    phase = arrange(delays)[None, :, :] * channel_ids[:, None, None] % chans
    angle = phase.astype(jnp.float32) * (2.0 * math.pi / chans)
    keep = flag_row[None, None, :] * (1.0 / math.sqrt(antennas))
    weights = jnp.concatenate(
        [
            jnp.cos(angle).astype(jnp.bfloat16) * keep.astype(jnp.bfloat16),
            jnp.sin(angle).astype(jnp.bfloat16) * keep.astype(jnp.bfloat16),
        ],
        axis=1,
    )
    beams = form_beams(blocks, weights)
    arranged = lax.all_to_all(beams, "chan", split_axis=0, concat_axis=0, tiled=True)
    arranged = arranged.reshape(devices, beam_count // devices, local_channels, 2 * spectra)
    visibilities = correlate(blocks, order, jnp.asarray(ids), flag_row)
    voltages = synthesize(arranged, proto, inverse)
    return visibilities, voltages


def solution(mesh):
    in_specs = (P(("groups", "chan"), None, None, None), P("groups"), P(), P("groups"))
    out_specs = (
        P(("groups", "chan"), None, None, None, None),
        P(("groups", "chan"), None, None, None),
    )
    return jax.shard_map(
        per_device, mesh=mesh, in_specs=in_specs, out_specs=out_specs, check_vma=False
    )
```

```python
import functools
import math

import jax
import jax.numpy as jnp
import ml_dtypes
import numpy as np
from jax import lax
from jax.experimental import pallas as pl
from jax.experimental.pallas import tpu as pltpu
from jax.sharding import PartitionSpec as P

TAPS = 16
TILE_ANTENNAS = 128
BLOCK_ANTENNAS = 16
FILTER_ANTENNAS = 8
BEAM_CHANNELS = 4
LANES = 128
VMEM_BYTES = 60 * 1024 * 1024


def prototype(tap_count, chan_count):
    length = tap_count * chan_count
    counter = np.arange(length, dtype=np.float32)
    shifted = (counter - np.float32((length - 1) / 2.0)) / np.float32(chan_count)
    window = 0.5 - 0.5 * np.cos(2.0 * math.pi * (counter + 0.5) / length)
    return (np.sinc(shifted) * window).astype(np.float32).reshape(tap_count, chan_count)


def dft_parts(chan_count):
    counter = np.arange(chan_count)
    angle = (counter[:, None] * counter[None, :] % chan_count) * (2.0 * math.pi / chan_count)
    return np.cos(angle), np.sin(angle)


def round_bf16(table):
    return table.astype(np.float32).astype(ml_dtypes.bfloat16)


def forward_table(chan_count):
    cosine, sine = dft_parts(chan_count)
    table = np.concatenate(
        [np.concatenate([cosine, sine], axis=1), np.concatenate([-sine, cosine], axis=1)], axis=0
    )
    return (round_bf16(table).astype(np.float32) / math.sqrt(chan_count)).astype(
        ml_dtypes.bfloat16
    )


def inverse_table(chan_count):
    cosine, sine = dft_parts(chan_count)
    table = np.concatenate(
        [np.concatenate([cosine, sine], axis=1), np.concatenate([-sine, cosine], axis=1)], axis=0
    )
    return (round_bf16(table).astype(np.float32) / math.sqrt(chan_count)).astype(
        ml_dtypes.bfloat16
    )


def channelize_kernel(samples_ref, proto_ref, table_ref, out_ref, planes, filtered, turned):
    chans, block, columns = out_ref.shape
    spectra = columns // 2
    lane_tiles = chans // LANES
    in_frames = spectra + TAPS - 1
    group = filtered.shape[1] // spectra
    words = 2 * lane_tiles
    rows = in_frames * words
    fold = turned.shape[2] // chans

    def convolve(step):
        planes[...] = samples_ref[step * group * rows : (step + 1) * group * rows, :].astype(jnp.float32)
        for member in range(group):
            for part in range(2):
                for tile in range(lane_tiles):
                    cols = slice(tile * LANES, (tile + 1) * LANES)
                    first = member * rows + 2 * tile + part
                    total = None
                    for tap in range(TAPS):
                        term = (
                            proto_ref[tap : tap + 1, cols]
                            * planes[pl.ds(first + tap * words, spectra, stride=words), :]
                        )
                        total = term if total is None else total + term
                    filtered[
                        step % 2,
                        member * spectra : (member + 1) * spectra,
                        part * chans + tile * LANES : part * chans + (tile + 1) * LANES,
                    ] = total.astype(jnp.bfloat16)

    def transform(step):
        product = lax.dot_general(
            table_ref[...],
            filtered[step % 2],
            (((1,), (1,)), ((), ())),
            preferred_element_type=jnp.float32,
        )
        for member in range(group):
            for part in range(2):
                ant = group * step + member
                turned[ant // fold, part, pl.ds(ant % fold, chans, stride=fold), :] = product[
                    part * chans : (part + 1) * chans, member * spectra : (member + 1) * spectra
                ]

    steps = block // group
    convolve(0)
    for step in range(steps):
        if step + 1 < steps:
            convolve(step + 1)
        transform(step)
    for part in range(2):
        pieces = [turned[i, part].reshape(chans, fold, spectra) for i in range(block // fold)]
        out_ref[:, :, part * spectra : (part + 1) * spectra] = jnp.concatenate(
            pieces, axis=1
        ).astype(jnp.bfloat16)


def channelize(samples, proto, table, first, count, block):
    antennas, _, in_frames, chans = samples.shape
    spectra = in_frames - TAPS + 1
    lane_tiles = chans // LANES
    rows = in_frames * lane_tiles * 2
    fold = 8 if block % 8 == 0 else block
    group = FILTER_ANTENNAS if block % FILTER_ANTENNAS == 0 else block
    flat = (
        samples.reshape(antennas, 2, in_frames, lane_tiles, LANES)
        .transpose(0, 2, 3, 1, 4)
        .reshape(antennas * rows, LANES)
    )
    return pl.pallas_call(
        channelize_kernel,
        grid=(count // block,),
        in_specs=[
            pl.BlockSpec((block * rows, LANES), lambda i: (i + first // block, 0)),
            pl.BlockSpec((TAPS, chans), lambda i: (0, 0)),
            pl.BlockSpec((2 * chans, 2 * chans), lambda i: (0, 0)),
        ],
        out_specs=pl.BlockSpec((chans, block, 2 * spectra), lambda i: (0, i, 0)),
        out_shape=jax.ShapeDtypeStruct((chans, count, 2 * spectra), jnp.bfloat16),
        scratch_shapes=[
            pltpu.VMEM((group * rows, LANES), jnp.float32),
            pltpu.VMEM((2, group * spectra, 2 * chans), jnp.bfloat16),
            pltpu.VMEM((block // fold, 2, chans * fold, spectra), jnp.float32),
        ],
        compiler_params=pltpu.CompilerParams(vmem_limit_bytes=VMEM_BYTES),
        cost_estimate=pl.CostEstimate(
            flops=count * spectra * 4 * chans * 2 * chans * 2,
            bytes_accessed=count * 2 * (in_frames + spectra) * chans * 2,
            transcendentals=0,
        ),
        name="channelize",
    )(flat, proto, table)


def beam_kernel(counts, *refs):
    x_refs = refs[: len(counts)]
    weights_ref, out_ref, turned = refs[len(counts) :]
    step = pl.program_id(0)
    beams, local, columns = out_ref.shape
    spectra = columns // 2
    group = weights_ref.shape[0]
    for member in range(group):
        product = None
        start = 0
        for x_ref, count in zip(x_refs, counts):
            term = jnp.dot(
                weights_ref[member, :, start : start + count],
                x_ref[:, member].reshape(count, columns),
                preferred_element_type=jnp.float32,
            )
            product = term if product is None else product + term
            start += count
        rows = pl.ds(step * group + member, beams, stride=local)
        turned[0, rows, :] = product[:beams, :spectra] + product[beams:, spectra:]
        turned[1, rows, :] = product[:beams, spectra:] - product[beams:, :spectra]

    @pl.when(step == pl.num_programs(0) - 1)
    def _():
        for part in range(2):
            out_ref[:, :, part * spectra : (part + 1) * spectra] = (
                turned[part].reshape(beams, local, spectra).astype(jnp.bfloat16)
            )


def form_beams(blocks, weights):
    local, double_beams, antennas = weights.shape
    beams = double_beams // 2
    columns = blocks[0].shape[3]
    counts = tuple(x.shape[0] * x.shape[2] for x in blocks)
    group = BEAM_CHANNELS if local % BEAM_CHANNELS == 0 else 1
    return pl.pallas_call(
        functools.partial(beam_kernel, counts),
        grid=(local // group,),
        in_specs=[
            pl.BlockSpec((x.shape[0], group, x.shape[2], columns), lambda c: (0, c, 0, 0))
            for x in blocks
        ]
        + [pl.BlockSpec((group, double_beams, antennas), lambda c: (c, 0, 0))],
        out_specs=pl.BlockSpec((beams, local, columns), lambda c: (0, 0, 0)),
        out_shape=jax.ShapeDtypeStruct((beams, local, columns), jnp.bfloat16),
        scratch_shapes=[pltpu.VMEM((2, beams * local, columns // 2), jnp.float32)],
        compiler_params=pltpu.CompilerParams(vmem_limit_bytes=VMEM_BYTES),
        cost_estimate=pl.CostEstimate(
            flops=2 * local * double_beams * antennas * columns,
            bytes_accessed=2 * local * (double_beams * antennas + antennas * columns + beams * columns),
            transcendentals=0,
        ),
        name="form_beams",
    )(*blocks, weights)


def visibility_kernel(counts, order_ref, ids_ref, flags_ref, *refs):
    x_refs = refs[: len(counts)]
    out_ref, select, permuted, turned = refs[len(counts) :]
    antennas, columns = permuted.shape
    spectra = columns // 2
    tile = TILE_ANTENNAS
    tiles = antennas // tile

    @pl.when(pl.program_id(0) == 0)
    def _():
        for t in range(tiles):
            rows = slice(t * tile, (t + 1) * tile)
            select[rows, :] = jnp.where(
                order_ref[rows, :] == ids_ref[...], flags_ref[...], 0.0
            ).astype(jnp.bfloat16)

    product = None
    start = 0
    for x_ref, count in zip(x_refs, counts):
        term = jnp.dot(
            select[:, start : start + count],
            x_ref[:, 0].reshape(count, columns),
            preferred_element_type=jnp.float32,
        )
        product = term if product is None else product + term
        start += count
    permuted[...] = product.astype(jnp.bfloat16)
    scaled = product * (1.0 / spectra)
    for t in range(tiles):
        block = scaled[t * tile : (t + 1) * tile, :]
        turned[2 * t * tile : (2 * t + 1) * tile, :] = block.astype(jnp.bfloat16)
        turned[(2 * t + 1) * tile : (2 * t + 2) * tile, :spectra] = block[:, spectra:].astype(jnp.bfloat16)
        turned[(2 * t + 1) * tile : (2 * t + 2) * tile, spectra:] = (-block[:, :spectra]).astype(jnp.bfloat16)
    pair = 0
    for p in range(tiles):
        left = turned[2 * p * tile : (2 * p + 2) * tile, :]
        result = lax.dot_general(
            left,
            permuted[p * tile :, :],
            (((1,), (1,)), ((), ())),
            preferred_element_type=jnp.float32,
        ).astype(jnp.bfloat16)
        for q in range(p, tiles):
            cols = slice((q - p) * tile, (q - p + 1) * tile)
            out_ref[0, pair, 0] = result[:tile, cols]
            out_ref[0, pair, 1] = result[tile:, cols]
            pair += 1


def correlate(blocks, order, ids, flags):
    antennas = order.shape[0]
    local, columns = blocks[0].shape[1], blocks[0].shape[3]
    counts = tuple(x.shape[0] * x.shape[2] for x in blocks)
    tiles = antennas // TILE_ANTENNAS
    pairs = tiles * (tiles + 1) // 2
    return pl.pallas_call(
        functools.partial(visibility_kernel, counts),
        grid=(local,),
        in_specs=[
            pl.BlockSpec((antennas, 1), lambda c: (0, 0)),
            pl.BlockSpec((1, antennas), lambda c: (0, 0)),
            pl.BlockSpec((1, antennas), lambda c: (0, 0)),
        ]
        + [
            pl.BlockSpec((x.shape[0], 1, x.shape[2], columns), lambda c: (0, c, 0, 0))
            for x in blocks
        ],
        out_specs=pl.BlockSpec(
            (1, pairs, 2, TILE_ANTENNAS, TILE_ANTENNAS), lambda c: (c, 0, 0, 0, 0)
        ),
        out_shape=jax.ShapeDtypeStruct(
            (local, pairs, 2, TILE_ANTENNAS, TILE_ANTENNAS), jnp.bfloat16
        ),
        scratch_shapes=[
            pltpu.VMEM((antennas, antennas), jnp.bfloat16),
            pltpu.VMEM((antennas, columns), jnp.bfloat16),
            pltpu.VMEM((2 * antennas, columns), jnp.bfloat16),
        ],
        compiler_params=pltpu.CompilerParams(vmem_limit_bytes=VMEM_BYTES),
        cost_estimate=pl.CostEstimate(
            flops=2 * local * columns * (antennas * antennas + pairs * 2 * TILE_ANTENNAS**2),
            bytes_accessed=2 * local * (antennas * columns + pairs * 2 * TILE_ANTENNAS**2),
            transcendentals=0,
        ),
        name="correlate",
    )(order[:, None], ids[None, :], flags[None, :], *blocks)


def synthesize_kernel(beams_ref, proto_ref, table_ref, out_ref, zeta, planes):
    sources, group, local, columns = beams_ref.shape
    chans = sources * local
    spectra = columns // 2
    lane_tiles = chans // LANES
    words = 2 * lane_tiles
    out_frames = planes.shape[0] // (group * words)
    for member in range(group):
        rows = beams_ref[:, member].reshape(chans, columns)
        for part in range(2):
            cols = slice(part * chans, (part + 1) * chans)
            value = None
            for source in range(2):
                term = lax.dot_general(
                    rows[:, source * spectra : (source + 1) * spectra],
                    table_ref[source * chans : (source + 1) * chans, cols],
                    (((0,), (0,)), ((), ())),
                    preferred_element_type=jnp.float32,
                )
                value = term if value is None else value + term
            value = value.astype(jnp.bfloat16).astype(jnp.float32)
            for tile in range(lane_tiles):
                lanes = slice(tile * LANES, (tile + 1) * LANES)
                zeta[...] = value[:, lanes]
                total = proto_ref[TAPS - 1 : TAPS, lanes] * zeta[pl.ds(0, out_frames), :]
                for tap in range(1, TAPS):
                    total = total + (
                        proto_ref[TAPS - 1 - tap : TAPS - tap, lanes]
                        * zeta[pl.ds(tap, out_frames), :]
                    )
                first = member * out_frames * words + 2 * tile + part
                planes[pl.ds(first, out_frames, stride=words), :] = total
    out_ref[...] = planes[...].astype(jnp.bfloat16)


def synthesize(arranged, proto, table):
    sources, beams, local, columns = arranged.shape
    chans = sources * local
    spectra = columns // 2
    lane_tiles = chans // LANES
    out_frames = spectra - TAPS + 1
    rows = out_frames * lane_tiles * 2
    group = 4 if beams % 4 == 0 else beams
    flat = pl.pallas_call(
        synthesize_kernel,
        grid=(beams // group,),
        in_specs=[
            pl.BlockSpec((sources, group, local, columns), lambda b: (0, b, 0, 0)),
            pl.BlockSpec((TAPS, chans), lambda b: (0, 0)),
            pl.BlockSpec((2 * chans, 2 * chans), lambda b: (0, 0)),
        ],
        out_specs=pl.BlockSpec((group * rows, LANES), lambda b: (b, 0)),
        out_shape=jax.ShapeDtypeStruct((beams * rows, LANES), jnp.bfloat16),
        scratch_shapes=[
            pltpu.VMEM((spectra, LANES), jnp.float32),
            pltpu.VMEM((group * rows, LANES), jnp.float32),
        ],
        compiler_params=pltpu.CompilerParams(vmem_limit_bytes=VMEM_BYTES),
        cost_estimate=pl.CostEstimate(
            flops=2 * beams * spectra * 4 * chans * chans,
            bytes_accessed=2 * beams * (columns + 2 * out_frames) * chans,
            transcendentals=0,
        ),
        name="synthesize",
    )(arranged, proto, table)
    return (
        flat.reshape(beams, out_frames, lane_tiles, 2, LANES)
        .transpose(0, 3, 1, 2, 4)
        .reshape(beams, 2, out_frames, chans)
    )


def per_device(samples, flags, delays, order):
    devices = lax.axis_size("chan")
    antennas_here, _, in_frames, chans = samples.shape
    local_channels = chans // devices
    spectra = in_frames - TAPS + 1
    antennas = antennas_here * devices
    beam_count = delays.shape[0]
    block = BLOCK_ANTENNAS if antennas_here % BLOCK_ANTENNAS == 0 else antennas_here
    sizes = [block, antennas_here - block] if antennas_here > block else [block]

    proto = jnp.asarray(prototype(TAPS, chans))
    forward = jnp.asarray(forward_table(chans))
    inverse = jnp.asarray(inverse_table(chans))

    blocks = []
    columns_of = []
    start = 0
    for size in sizes:
        part = channelize(samples, proto, forward, start, size, block)
        part = lax.all_to_all(part, "chan", split_axis=0, concat_axis=0, tiled=True)
        blocks.append(part.reshape(devices, local_channels, size, 2 * spectra))
        ids = np.arange(antennas, dtype=np.int32).reshape(devices, antennas_here)
        columns_of.append(ids[:, start : start + size].reshape(-1))
        start += size
    ids = np.concatenate(columns_of)

    def arrange(x):
        x = x.reshape(x.shape[:-1] + (devices, antennas_here))
        pieces = []
        at = 0
        for size in sizes:
            pieces.append(x[..., at : at + size].reshape(x.shape[:-2] + (devices * size,)))
            at += size
        return jnp.concatenate(pieces, axis=-1)

    flag_row = arrange(flags).astype(jnp.float32)
    channel_ids = lax.axis_index("chan") * local_channels + jnp.arange(
        local_channels, dtype=jnp.int32
    )
    phase = arrange(delays)[None, :, :] * channel_ids[:, None, None] % chans
    angle = phase.astype(jnp.float32) * (2.0 * math.pi / chans)
    keep = flag_row[None, None, :] * (1.0 / math.sqrt(antennas))
    weights = jnp.concatenate(
        [
            jnp.cos(angle).astype(jnp.bfloat16) * keep.astype(jnp.bfloat16),
            jnp.sin(angle).astype(jnp.bfloat16) * keep.astype(jnp.bfloat16),
        ],
        axis=1,
    )
    beams = form_beams(blocks, weights)
    arranged = lax.all_to_all(beams, "chan", split_axis=0, concat_axis=0, tiled=True)
    arranged = arranged.reshape(devices, beam_count // devices, local_channels, 2 * spectra)
    visibilities = correlate(blocks, order, jnp.asarray(ids), flag_row)
    voltages = synthesize(arranged, proto, inverse)
    return visibilities, voltages


def solution(mesh):
    in_specs = (P(("groups", "chan"), None, None, None), P("groups"), P(), P("groups"))
    out_specs = (
        P(("groups", "chan"), None, None, None, None),
        P(("groups", "chan"), None, None, None),
    )
    return jax.shard_map(
        per_device, mesh=mesh, in_specs=in_specs, out_specs=out_specs, check_vma=False
    )
```

```python
import functools
import math

import jax
import jax.numpy as jnp
import ml_dtypes
import numpy as np
from jax import lax
from jax.experimental import pallas as pl
from jax.experimental.pallas import tpu as pltpu
from jax.sharding import PartitionSpec as P


TAPS = 16
TILE_ANTENNAS = 128
CHUNK_ANTENNAS = 16
FILTER_ANTENNAS = 8
BEAM_CHANNELS = 4
LANES = 128
VMEM_BYTES = 60 * 1024 * 1024


def prototype(tap_count, chan_count):
    length = tap_count * chan_count
    counter = np.arange(length, dtype=np.float32)
    shifted = (counter - np.float32((length - 1) / 2.0)) / np.float32(chan_count)
    window = 0.5 - 0.5 * np.cos(2.0 * math.pi * (counter + 0.5) / length)
    return (np.sinc(shifted) * window).astype(np.float32).reshape(tap_count, chan_count)


def dft_parts(chan_count):
    counter = np.arange(chan_count)
    angle = (counter[:, None] * counter[None, :] % chan_count) * (2.0 * math.pi / chan_count)
    return np.cos(angle), np.sin(angle)


def round_bf16(table):
    return table.astype(np.float32).astype(ml_dtypes.bfloat16)


def transform_table(chan_count):
    cosine, sine = dft_parts(chan_count)
    table = np.concatenate(
        [np.concatenate([cosine, sine], axis=1), np.concatenate([-sine, cosine], axis=1)], axis=0
    )
    return (round_bf16(table).astype(np.float32) / math.sqrt(chan_count)).astype(
        ml_dtypes.bfloat16
    )


def channelize_kernel(samples_ref, proto_ref, table_ref, out_ref, planes, filtered, turned):
    chans, block, columns = out_ref.shape
    spectra = columns // 2
    lane_tiles = chans // LANES
    in_frames = spectra + TAPS - 1
    group = filtered.shape[1] // spectra
    words = 2 * lane_tiles
    rows = in_frames * words
    fold = turned.shape[2] // chans

    def convolve(step):
        planes[...] = samples_ref[step * group * rows : (step + 1) * group * rows, :].astype(jnp.float32)
        for member in range(group):
            for part in range(2):
                for tile in range(lane_tiles):
                    cols = slice(tile * LANES, (tile + 1) * LANES)
                    first = member * rows + 2 * tile + part
                    total = None
                    for tap in range(TAPS):
                        term = (
                            proto_ref[tap : tap + 1, cols]
                            * planes[pl.ds(first + tap * words, spectra, stride=words), :]
                        )
                        total = term if total is None else total + term
                    filtered[
                        step % 2,
                        member * spectra : (member + 1) * spectra,
                        part * chans + tile * LANES : part * chans + (tile + 1) * LANES,
                    ] = total.astype(jnp.bfloat16)

    def transform(step):
        product = lax.dot_general(
            table_ref[...],
            filtered[step % 2],
            (((1,), (1,)), ((), ())),
            preferred_element_type=jnp.float32,
        )
        for member in range(group):
            for part in range(2):
                ant = group * step + member
                turned[ant // fold, part, pl.ds(ant % fold, chans, stride=fold), :] = product[
                    part * chans : (part + 1) * chans, member * spectra : (member + 1) * spectra
                ]

    steps = block // group
    convolve(0)
    for step in range(steps):
        if step + 1 < steps:
            convolve(step + 1)
        transform(step)
    for part in range(2):
        pieces = [turned[i, part].reshape(chans, fold, spectra) for i in range(block // fold)]
        out_ref[:, :, part * spectra : (part + 1) * spectra] = jnp.concatenate(
            pieces, axis=1
        ).astype(jnp.bfloat16)


def channelize(samples, proto, table, first, count):
    antennas, _, in_frames, chans = samples.shape
    spectra = in_frames - TAPS + 1
    lane_tiles = chans // LANES
    rows = in_frames * lane_tiles * 2
    block = FILTER_ANTENNAS if count % FILTER_ANTENNAS == 0 and first % FILTER_ANTENNAS == 0 else count
    fold = block
    group = block
    flat = (
        samples.reshape(antennas, 2, in_frames, lane_tiles, LANES)
        .transpose(0, 2, 3, 1, 4)
        .reshape(antennas * rows, LANES)
    )
    return pl.pallas_call(
        channelize_kernel,
        grid=(count // block,),
        in_specs=[
            pl.BlockSpec((block * rows, LANES), lambda i: (i + first // block, 0)),
            pl.BlockSpec((TAPS, chans), lambda i: (0, 0)),
            pl.BlockSpec((2 * chans, 2 * chans), lambda i: (0, 0)),
        ],
        out_specs=pl.BlockSpec((chans, block, 2 * spectra), lambda i: (0, i, 0)),
        out_shape=jax.ShapeDtypeStruct((chans, count, 2 * spectra), jnp.bfloat16),
        scratch_shapes=[
            pltpu.VMEM((group * rows, LANES), jnp.float32),
            pltpu.VMEM((2, group * spectra, 2 * chans), jnp.bfloat16),
            pltpu.VMEM((block // fold, 2, chans * fold, spectra), jnp.float32),
        ],
        compiler_params=pltpu.CompilerParams(vmem_limit_bytes=VMEM_BYTES),
        cost_estimate=pl.CostEstimate(
            flops=count * spectra * 4 * chans * 2 * chans * 2,
            bytes_accessed=count * 2 * (in_frames + spectra) * chans * 2,
            transcendentals=0,
        ),
        name="channelize",
    )(flat, proto, table)


def beam_kernel(counts, *refs):
    x_refs = refs[: len(counts)]
    weights_ref, out_ref, turned = refs[len(counts) :]
    step = pl.program_id(0)
    beams, local, columns = out_ref.shape
    spectra = columns // 2
    group = weights_ref.shape[0]
    for member in range(group):
        product = None
        start = 0
        for x_ref, count in zip(x_refs, counts):
            term = jnp.dot(
                weights_ref[member, :, start : start + count],
                x_ref[:, member].reshape(count, columns),
                preferred_element_type=jnp.float32,
            )
            product = term if product is None else product + term
            start += count
        rows = pl.ds(step * group + member, beams, stride=local)
        turned[0, rows, :] = product[:beams, :spectra] + product[beams:, spectra:]
        turned[1, rows, :] = product[:beams, spectra:] - product[beams:, :spectra]

    @pl.when(step == pl.num_programs(0) - 1)
    def _():
        for part in range(2):
            out_ref[:, :, part * spectra : (part + 1) * spectra] = (
                turned[part].reshape(beams, local, spectra).astype(jnp.bfloat16)
            )


def form_beams(blocks, weights):
    local, double_beams, antennas = weights.shape
    beams = double_beams // 2
    columns = blocks[0].shape[3]
    counts = tuple(x.shape[0] * x.shape[2] for x in blocks)
    group = BEAM_CHANNELS if local % BEAM_CHANNELS == 0 else 1
    return pl.pallas_call(
        functools.partial(beam_kernel, counts),
        grid=(local // group,),
        in_specs=[
            pl.BlockSpec((x.shape[0], group, x.shape[2], columns), lambda c: (0, c, 0, 0))
            for x in blocks
        ]
        + [pl.BlockSpec((group, double_beams, antennas), lambda c: (c, 0, 0))],
        out_specs=pl.BlockSpec((beams, local, columns), lambda c: (0, 0, 0)),
        out_shape=jax.ShapeDtypeStruct((beams, local, columns), jnp.bfloat16),
        scratch_shapes=[pltpu.VMEM((2, beams * local, columns // 2), jnp.float32)],
        compiler_params=pltpu.CompilerParams(vmem_limit_bytes=VMEM_BYTES),
        cost_estimate=pl.CostEstimate(
            flops=2 * local * double_beams * antennas * columns,
            bytes_accessed=2 * local * (double_beams * antennas + antennas * columns + beams * columns),
            transcendentals=0,
        ),
        name="form_beams",
    )(*blocks, weights)


def visibility_kernel(counts, order_ref, ids_ref, flags_ref, *refs):
    x_refs = refs[: len(counts)]
    out_ref, select, permuted, turned = refs[len(counts) :]
    antennas, columns = permuted.shape
    spectra = columns // 2
    tile = TILE_ANTENNAS
    tiles = antennas // tile

    @pl.when(pl.program_id(0) == 0)
    def _():
        def fill(t, carry):
            rows = pl.ds(pl.multiple_of(t * tile, tile), tile)
            select[rows, :] = jnp.where(
                order_ref[rows, :] == ids_ref[...], flags_ref[...], 0.0
            ).astype(jnp.bfloat16)
            return carry

        lax.fori_loop(0, tiles, fill, 0)

    product = None
    start = 0
    for x_ref, count in zip(x_refs, counts):
        term = jnp.dot(
            select[:, start : start + count],
            x_ref[:, 0].reshape(count, columns),
            preferred_element_type=jnp.float32,
        )
        product = term if product is None else product + term
        start += count
    permuted[...] = product.astype(jnp.bfloat16)
    scaled = product * (1.0 / spectra)
    for t in range(tiles):
        block = scaled[t * tile : (t + 1) * tile, :]
        turned[2 * t * tile : (2 * t + 1) * tile, :] = block.astype(jnp.bfloat16)
        turned[(2 * t + 1) * tile : (2 * t + 2) * tile, :spectra] = block[:, spectra:].astype(jnp.bfloat16)
        turned[(2 * t + 1) * tile : (2 * t + 2) * tile, spectra:] = (-block[:, :spectra]).astype(jnp.bfloat16)
    pair = 0
    for p in range(tiles):
        left = turned[2 * p * tile : (2 * p + 2) * tile, :]
        result = lax.dot_general(
            left,
            permuted[p * tile :, :],
            (((1,), (1,)), ((), ())),
            preferred_element_type=jnp.float32,
        ).astype(jnp.bfloat16)
        for q in range(p, tiles):
            cols = slice((q - p) * tile, (q - p + 1) * tile)
            out_ref[0, pair, 0] = result[:tile, cols]
            out_ref[0, pair, 1] = result[tile:, cols]
            pair += 1


def correlate(blocks, order, ids, flags):
    antennas = order.shape[0]
    local, columns = blocks[0].shape[1], blocks[0].shape[3]
    counts = tuple(x.shape[0] * x.shape[2] for x in blocks)
    tiles = antennas // TILE_ANTENNAS
    pairs = tiles * (tiles + 1) // 2
    return pl.pallas_call(
        functools.partial(visibility_kernel, counts),
        grid=(local,),
        in_specs=[
            pl.BlockSpec((antennas, 1), lambda c: (0, 0)),
            pl.BlockSpec((1, antennas), lambda c: (0, 0)),
            pl.BlockSpec((1, antennas), lambda c: (0, 0)),
        ]
        + [
            pl.BlockSpec((x.shape[0], 1, x.shape[2], columns), lambda c: (0, c, 0, 0))
            for x in blocks
        ],
        out_specs=pl.BlockSpec(
            (1, pairs, 2, TILE_ANTENNAS, TILE_ANTENNAS), lambda c: (c, 0, 0, 0, 0)
        ),
        out_shape=jax.ShapeDtypeStruct(
            (local, pairs, 2, TILE_ANTENNAS, TILE_ANTENNAS), jnp.bfloat16
        ),
        scratch_shapes=[
            pltpu.VMEM((antennas, antennas), jnp.bfloat16),
            pltpu.VMEM((antennas, columns), jnp.bfloat16),
            pltpu.VMEM((2 * antennas, columns), jnp.bfloat16),
        ],
        compiler_params=pltpu.CompilerParams(vmem_limit_bytes=VMEM_BYTES),
        cost_estimate=pl.CostEstimate(
            flops=2 * local * columns * (antennas * antennas + pairs * 2 * TILE_ANTENNAS**2),
            bytes_accessed=2 * local * (antennas * columns + pairs * 2 * TILE_ANTENNAS**2),
            transcendentals=0,
        ),
        name="correlate",
    )(order[:, None], ids[None, :], flags[None, :], *blocks)


def synthesize_kernel(beams_ref, proto_ref, table_ref, out_ref, zeta, planes):
    sources, group, local, columns = beams_ref.shape
    chans = sources * local
    spectra = columns // 2
    lane_tiles = chans // LANES
    words = 2 * lane_tiles
    out_frames = planes.shape[0] // (group * words)
    for member in range(group):
        rows = beams_ref[:, member].reshape(chans, columns)
        for part in range(2):
            cols = slice(part * chans, (part + 1) * chans)
            value = None
            for source in range(2):
                term = lax.dot_general(
                    rows[:, source * spectra : (source + 1) * spectra],
                    table_ref[source * chans : (source + 1) * chans, cols],
                    (((0,), (0,)), ((), ())),
                    preferred_element_type=jnp.float32,
                )
                value = term if value is None else value + term
            value = value.astype(jnp.bfloat16).astype(jnp.float32)
            for tile in range(lane_tiles):
                lanes = slice(tile * LANES, (tile + 1) * LANES)
                zeta[...] = value[:, lanes]
                total = proto_ref[TAPS - 1 : TAPS, lanes] * zeta[pl.ds(0, out_frames), :]
                for tap in range(1, TAPS):
                    total = total + (
                        proto_ref[TAPS - 1 - tap : TAPS - tap, lanes]
                        * zeta[pl.ds(tap, out_frames), :]
                    )
                first = member * out_frames * words + 2 * tile + part
                planes[pl.ds(first, out_frames, stride=words), :] = total
    out_ref[...] = planes[...].astype(jnp.bfloat16)


def synthesize(arranged, proto, table):
    sources, beams, local, columns = arranged.shape
    chans = sources * local
    spectra = columns // 2
    lane_tiles = chans // LANES
    out_frames = spectra - TAPS + 1
    rows = out_frames * lane_tiles * 2
    group = 4 if beams % 4 == 0 else beams
    flat = pl.pallas_call(
        synthesize_kernel,
        grid=(beams // group,),
        in_specs=[
            pl.BlockSpec((sources, group, local, columns), lambda b: (0, b, 0, 0)),
            pl.BlockSpec((TAPS, chans), lambda b: (0, 0)),
            pl.BlockSpec((2 * chans, 2 * chans), lambda b: (0, 0)),
        ],
        out_specs=pl.BlockSpec((group * rows, LANES), lambda b: (b, 0)),
        out_shape=jax.ShapeDtypeStruct((beams * rows, LANES), jnp.bfloat16),
        scratch_shapes=[
            pltpu.VMEM((spectra, LANES), jnp.float32),
            pltpu.VMEM((group * rows, LANES), jnp.float32),
        ],
        compiler_params=pltpu.CompilerParams(vmem_limit_bytes=VMEM_BYTES),
        cost_estimate=pl.CostEstimate(
            flops=2 * beams * spectra * 4 * chans * chans,
            bytes_accessed=2 * beams * (columns + 2 * out_frames) * chans,
            transcendentals=0,
        ),
        name="synthesize",
    )(arranged, proto, table)
    return (
        flat.reshape(beams, out_frames, lane_tiles, 2, LANES)
        .transpose(0, 3, 1, 2, 4)
        .reshape(beams, 2, out_frames, chans)
    )


def turn(part):
    return lax.all_to_all(part, "chan", split_axis=0, concat_axis=0, tiled=True)


def exchange_early(first, second):
    devices = lax.axis_size("chan")
    me = lax.axis_index("chan")
    chans = first.shape[0]

    def send(source, mask):
        split = source.reshape((devices, chans // devices) + source.shape[1:])
        mine = lax.dynamic_index_in_dim(split, me ^ mask, 0, keepdims=False)
        if mask == 0:
            return mine
        return lax.ppermute(mine, "chan", [(i, i ^ mask) for i in range(devices)])

    far = [mask for mask in range(devices // 2, devices)]
    near = [mask for mask in range(devices // 2)]
    got = {mask: send(first, mask) for mask in far}
    late, second = lax.optimization_barrier((first, second))
    rest = turn(second)
    got.update({mask: send(late, mask) for mask in near})
    stacked = jnp.stack([got[mask] for mask in range(devices)])
    ordered = [
        lax.dynamic_index_in_dim(stacked, me ^ source, 0, keepdims=False)
        for source in range(devices)
    ]
    return jnp.concatenate(ordered, axis=0), rest


def per_device(samples, flags, delays, order):
    devices = lax.axis_size("chan")
    antennas_here, _, in_frames, chans = samples.shape
    local_channels = chans // devices
    spectra = in_frames - TAPS + 1
    antennas = antennas_here * devices
    beam_count = delays.shape[0]
    block = CHUNK_ANTENNAS if antennas_here > CHUNK_ANTENNAS else antennas_here
    sizes = [block, antennas_here - block] if antennas_here > block else [block]

    proto = jnp.asarray(prototype(TAPS, chans))
    table = jnp.asarray(transform_table(chans))

    parts = []
    columns_of = []
    start = 0
    for size in sizes:
        parts.append(channelize(samples, proto, table, start, size))
        ids = np.arange(antennas, dtype=np.int32).reshape(devices, antennas_here)
        columns_of.append(ids[:, start : start + size].reshape(-1))
        start += size
    ids = np.concatenate(columns_of)
    if len(parts) > 1:
        early, rest = exchange_early(parts[0], parts[1])
        parts = [early, rest]
    else:
        parts = [turn(parts[0])]
    blocks = [
        x.reshape(devices, local_channels, size, 2 * spectra) for x, size in zip(parts, sizes)
    ]

    def arrange(x):
        x = x.reshape(x.shape[:-1] + (devices, antennas_here))
        pieces = []
        at = 0
        for size in sizes:
            pieces.append(x[..., at : at + size].reshape(x.shape[:-2] + (devices * size,)))
            at += size
        return jnp.concatenate(pieces, axis=-1)

    flag_row = arrange(flags).astype(jnp.float32)
    channel_ids = lax.axis_index("chan") * local_channels + jnp.arange(
        local_channels, dtype=jnp.int32
    )
    phase = arrange(delays)[None, :, :] * channel_ids[:, None, None] % chans
    angle = phase.astype(jnp.float32) * (2.0 * math.pi / chans)
    keep = flag_row[None, None, :] * (1.0 / math.sqrt(antennas))
    weights = jnp.concatenate(
        [
            jnp.cos(angle).astype(jnp.bfloat16) * keep.astype(jnp.bfloat16),
            jnp.sin(angle).astype(jnp.bfloat16) * keep.astype(jnp.bfloat16),
        ],
        axis=1,
    )
    beams = form_beams(blocks, weights)
    arranged = turn(beams)
    arranged = arranged.reshape(devices, beam_count // devices, local_channels, 2 * spectra)
    visibilities = correlate(blocks, order, jnp.asarray(ids), flag_row)
    voltages = synthesize(arranged, proto, table)
    return visibilities, voltages


def solution(mesh):
    in_specs = (P(("groups", "chan"), None, None, None), P("groups"), P(), P("groups"))
    out_specs = (
        P(("groups", "chan"), None, None, None, None),
        P(("groups", "chan"), None, None, None),
    )

    return jax.shard_map(
        per_device, mesh=mesh, in_specs=in_specs, out_specs=out_specs, check_vma=False
    )
```

```python
import functools
import math

import jax
import jax.numpy as jnp
import ml_dtypes
import numpy as np
from jax import lax
from jax.experimental import pallas as pl
from jax.experimental.pallas import tpu as pltpu
from jax.sharding import PartitionSpec as P


TAPS = 16
TILE_ANTENNAS = 128
CHUNK_ANTENNAS = 16
FILTER_ANTENNAS = 8
LANES = 128
VMEM_BYTES = 60 * 1024 * 1024


def prototype(tap_count, chan_count):
    length = tap_count * chan_count
    counter = np.arange(length, dtype=np.float32)
    shifted = (counter - np.float32((length - 1) / 2.0)) / np.float32(chan_count)
    window = 0.5 - 0.5 * np.cos(2.0 * math.pi * (counter + 0.5) / length)
    return (np.sinc(shifted) * window).astype(np.float32).reshape(tap_count, chan_count)


def dft_parts(chan_count):
    counter = np.arange(chan_count)
    angle = (counter[:, None] * counter[None, :] % chan_count) * (2.0 * math.pi / chan_count)
    return np.cos(angle), np.sin(angle)


def round_bf16(table):
    return table.astype(np.float32).astype(ml_dtypes.bfloat16)


def transform_table(chan_count):
    cosine, sine = dft_parts(chan_count)
    table = np.concatenate(
        [np.concatenate([cosine, sine], axis=1), np.concatenate([-sine, cosine], axis=1)], axis=0
    )
    return (round_bf16(table).astype(np.float32) / math.sqrt(chan_count)).astype(
        ml_dtypes.bfloat16
    )


def channelize_kernel(samples_ref, proto_ref, table_ref, out_ref, planes, filtered, turned):
    chans, block, columns = out_ref.shape
    spectra = columns // 2
    lane_tiles = chans // LANES
    in_frames = spectra + TAPS - 1
    group = filtered.shape[1] // spectra
    words = 2 * lane_tiles
    rows = in_frames * words
    fold = turned.shape[2] // chans

    def convolve(step):
        planes[...] = samples_ref[step * group * rows : (step + 1) * group * rows, :].astype(jnp.float32)
        for member in range(group):
            for part in range(2):
                for tile in range(lane_tiles):
                    cols = slice(tile * LANES, (tile + 1) * LANES)
                    first = member * rows + 2 * tile + part
                    total = None
                    for tap in range(TAPS):
                        term = (
                            proto_ref[tap : tap + 1, cols]
                            * planes[pl.ds(first + tap * words, spectra, stride=words), :]
                        )
                        total = term if total is None else total + term
                    filtered[
                        step % 2,
                        member * spectra : (member + 1) * spectra,
                        part * chans + tile * LANES : part * chans + (tile + 1) * LANES,
                    ] = total.astype(jnp.bfloat16)

    def transform(step):
        product = lax.dot_general(
            table_ref[...],
            filtered[step % 2],
            (((1,), (1,)), ((), ())),
            preferred_element_type=jnp.float32,
        )
        for member in range(group):
            for part in range(2):
                ant = group * step + member
                turned[ant // fold, part, pl.ds(ant % fold, chans, stride=fold), :] = product[
                    part * chans : (part + 1) * chans, member * spectra : (member + 1) * spectra
                ]

    steps = block // group
    convolve(0)
    for step in range(steps):
        if step + 1 < steps:
            convolve(step + 1)
        transform(step)
    for part in range(2):
        pieces = [turned[i, part].reshape(chans, fold, spectra) for i in range(block // fold)]
        out_ref[:, :, part * spectra : (part + 1) * spectra] = jnp.concatenate(
            pieces, axis=1
        ).astype(jnp.bfloat16)


def channelize(samples, proto, table, first, count):
    antennas, _, in_frames, chans = samples.shape
    spectra = in_frames - TAPS + 1
    lane_tiles = chans // LANES
    rows = in_frames * lane_tiles * 2
    block = FILTER_ANTENNAS if count % FILTER_ANTENNAS == 0 and first % FILTER_ANTENNAS == 0 else count
    fold = block
    group = block
    flat = (
        samples.reshape(antennas, 2, in_frames, lane_tiles, LANES)
        .transpose(0, 2, 3, 1, 4)
        .reshape(antennas * rows, LANES)
    )
    return pl.pallas_call(
        channelize_kernel,
        grid=(count // block,),
        in_specs=[
            pl.BlockSpec((block * rows, LANES), lambda i: (i + first // block, 0)),
            pl.BlockSpec((TAPS, chans), lambda i: (0, 0)),
            pl.BlockSpec((2 * chans, 2 * chans), lambda i: (0, 0)),
        ],
        out_specs=pl.BlockSpec((chans, block, 2 * spectra), lambda i: (0, i, 0)),
        out_shape=jax.ShapeDtypeStruct((chans, count, 2 * spectra), jnp.bfloat16),
        scratch_shapes=[
            pltpu.VMEM((group * rows, LANES), jnp.float32),
            pltpu.VMEM((2, group * spectra, 2 * chans), jnp.bfloat16),
            pltpu.VMEM((block // fold, 2, chans * fold, spectra), jnp.float32),
        ],
        compiler_params=pltpu.CompilerParams(vmem_limit_bytes=VMEM_BYTES),
        cost_estimate=pl.CostEstimate(
            flops=count * spectra * 4 * chans * 2 * chans * 2,
            bytes_accessed=count * 2 * (in_frames + spectra) * chans * 2,
            transcendentals=0,
        ),
        name="channelize",
    )(flat, proto, table)


def weights_kernel(start_cos, start_sin, turn_cos, turn_sin, keep_ref, out_ref, cosine, sine):
    local, double_beams, _ = out_ref.shape
    beams = double_beams // 2
    rows = 8 if beams % 8 == 0 else beams
    cosine[...] = start_cos[...]
    sine[...] = start_sin[...]

    def channel(c, carry):
        def strip(i, inner):
            here = pl.ds(pl.multiple_of(i * 2 * rows, 2 * rows), 2 * rows)
            there = pl.ds(pl.multiple_of(i * 2 * rows + beams, 2 * rows), 2 * rows)
            co, si = cosine[here, :], sine[here, :]
            tc, ts = turn_cos[here, :], turn_sin[here, :]
            out_ref[c, here, :] = (co * keep_ref[...]).astype(jnp.bfloat16)
            out_ref[c, there, :] = (si * keep_ref[...]).astype(jnp.bfloat16)
            cosine[here, :] = co * tc - si * ts
            sine[here, :] = si * tc + co * ts
            return inner

        return lax.fori_loop(0, beams // (2 * rows), strip, carry)

    lax.fori_loop(0, local, channel, 0)


def make_weights(delays, keep, first_channel, local, chans):
    beams, antennas = delays.shape
    step = 2.0 * math.pi / chans
    start = (delays * first_channel % chans).astype(jnp.float32) * step
    turns = delays.astype(jnp.float32) * step
    vmem = pl.BlockSpec(memory_space=pltpu.VMEM)
    return pl.pallas_call(
        weights_kernel,
        in_specs=[vmem] * 5,
        out_specs=vmem,
        out_shape=jax.ShapeDtypeStruct((local, 2 * beams, antennas), jnp.bfloat16),
        scratch_shapes=[pltpu.VMEM((beams, antennas), jnp.float32)] * 2,
        compiler_params=pltpu.CompilerParams(vmem_limit_bytes=40 * 1024 * 1024),
        cost_estimate=pl.CostEstimate(
            flops=10 * local * beams * antennas,
            bytes_accessed=4 * 4 * beams * antennas + 4 * local * beams * antennas,
            transcendentals=0,
        ),
        name="make_weights",
    )(jnp.cos(start), jnp.sin(start), jnp.cos(turns), jnp.sin(turns), keep)


def beam_kernel(counts, *refs):
    kinds = len(counts) + 1
    sources, (out_ref, turned), holds, sems = (
        refs[:kinds], refs[kinds : kinds + 2], refs[kinds + 2 : -1], refs[-1]
    )
    beams, local, columns = out_ref.shape
    spectra = columns // 2

    def copies(channel):
        views = [x.at[:, channel] for x in sources[:-1]] + [sources[-1].at[channel]]
        return [
            pltpu.make_async_copy(view, hold.at[channel], sems.at[kind, channel])
            for kind, (view, hold) in enumerate(zip(views, holds))
        ]

    def begin(channel, carry):
        for copy in copies(channel):
            copy.start()
        return carry

    lax.fori_loop(0, local, begin, 0)

    def form(channel, carry):
        for copy in copies(channel):
            copy.wait()
        product = None
        start = 0
        for hold, count in zip(holds, counts):
            term = jnp.dot(
                holds[-1][channel, :, start : start + count],
                hold[channel].reshape(count, columns),
                preferred_element_type=jnp.float32,
            )
            product = term if product is None else product + term
            start += count
        rows = pl.ds(channel, beams, stride=local)
        turned[0, rows, :] = product[:beams, :spectra] + product[beams:, spectra:]
        turned[1, rows, :] = product[:beams, spectra:] - product[beams:, :spectra]
        return carry

    lax.fori_loop(0, local, form, 0)
    for part in range(2):
        out_ref[:, :, part * spectra : (part + 1) * spectra] = (
            turned[part].reshape(beams, local, spectra).astype(jnp.bfloat16)
        )


def form_beams(blocks, weights):
    local, double_beams, antennas = weights.shape
    beams = double_beams // 2
    columns = blocks[0].shape[3]
    counts = tuple(x.shape[0] * x.shape[2] for x in blocks)
    return pl.pallas_call(
        functools.partial(beam_kernel, counts),
        in_specs=[pl.BlockSpec(memory_space=pl.ANY)] * (len(blocks) + 1),
        out_specs=pl.BlockSpec(memory_space=pltpu.VMEM),
        out_shape=jax.ShapeDtypeStruct((beams, local, columns), jnp.bfloat16),
        scratch_shapes=[pltpu.VMEM((2, beams * local, columns // 2), jnp.float32)]
        + [pltpu.VMEM((local, x.shape[0], x.shape[2], columns), jnp.bfloat16) for x in blocks]
        + [
            pltpu.VMEM((local, double_beams, antennas), jnp.bfloat16),
            pltpu.SemaphoreType.DMA((len(blocks) + 1, local)),
        ],
        compiler_params=pltpu.CompilerParams(vmem_limit_bytes=VMEM_BYTES),
        cost_estimate=pl.CostEstimate(
            flops=2 * local * double_beams * antennas * columns,
            bytes_accessed=2 * local * (double_beams * antennas + antennas * columns + beams * columns),
            transcendentals=0,
        ),
        name="form_beams",
    )(*blocks, weights)


def visibility_kernel(counts, order_ref, ids_ref, flags_ref, *refs):
    x_refs = refs[: len(counts)]
    out_ref, select, permuted, turned = refs[len(counts) :]
    antennas, columns = permuted.shape
    spectra = columns // 2
    tile = TILE_ANTENNAS
    tiles = antennas // tile

    @pl.when(pl.program_id(0) == 0)
    def _():
        def fill(t, carry):
            rows = pl.ds(pl.multiple_of(t * tile, tile), tile)
            select[rows, :] = jnp.where(
                order_ref[rows, :] == ids_ref[...], flags_ref[...], 0.0
            ).astype(jnp.bfloat16)
            return carry

        lax.fori_loop(0, tiles, fill, 0)

    product = None
    start = 0
    for x_ref, count in zip(x_refs, counts):
        term = jnp.dot(
            select[:, start : start + count],
            x_ref[:, 0].reshape(count, columns),
            preferred_element_type=jnp.float32,
        )
        product = term if product is None else product + term
        start += count
    permuted[...] = product.astype(jnp.bfloat16)
    scaled = product * (1.0 / spectra)
    for t in range(tiles):
        block = scaled[t * tile : (t + 1) * tile, :]
        turned[2 * t * tile : (2 * t + 1) * tile, :] = block.astype(jnp.bfloat16)
        turned[(2 * t + 1) * tile : (2 * t + 2) * tile, :spectra] = block[:, spectra:].astype(jnp.bfloat16)
        turned[(2 * t + 1) * tile : (2 * t + 2) * tile, spectra:] = (-block[:, :spectra]).astype(jnp.bfloat16)
    pair = 0
    for p in range(tiles):
        left = turned[2 * p * tile : (2 * p + 2) * tile, :]
        result = lax.dot_general(
            left,
            permuted[p * tile :, :],
            (((1,), (1,)), ((), ())),
            preferred_element_type=jnp.float32,
        ).astype(jnp.bfloat16)
        for q in range(p, tiles):
            cols = slice((q - p) * tile, (q - p + 1) * tile)
            out_ref[0, pair, 0] = result[:tile, cols]
            out_ref[0, pair, 1] = result[tile:, cols]
            pair += 1


def correlate(blocks, order, ids, flags):
    antennas = order.shape[0]
    local, columns = blocks[0].shape[1], blocks[0].shape[3]
    counts = tuple(x.shape[0] * x.shape[2] for x in blocks)
    tiles = antennas // TILE_ANTENNAS
    pairs = tiles * (tiles + 1) // 2
    return pl.pallas_call(
        functools.partial(visibility_kernel, counts),
        grid=(local,),
        in_specs=[
            pl.BlockSpec((antennas, 1), lambda c: (0, 0)),
            pl.BlockSpec((1, antennas), lambda c: (0, 0)),
            pl.BlockSpec((1, antennas), lambda c: (0, 0)),
        ]
        + [
            pl.BlockSpec((x.shape[0], 1, x.shape[2], columns), lambda c: (0, c, 0, 0))
            for x in blocks
        ],
        out_specs=pl.BlockSpec(
            (1, pairs, 2, TILE_ANTENNAS, TILE_ANTENNAS), lambda c: (c, 0, 0, 0, 0)
        ),
        out_shape=jax.ShapeDtypeStruct(
            (local, pairs, 2, TILE_ANTENNAS, TILE_ANTENNAS), jnp.bfloat16
        ),
        scratch_shapes=[
            pltpu.VMEM((antennas, antennas), jnp.bfloat16),
            pltpu.VMEM((antennas, columns), jnp.bfloat16),
            pltpu.VMEM((2 * antennas, columns), jnp.bfloat16),
        ],
        compiler_params=pltpu.CompilerParams(vmem_limit_bytes=VMEM_BYTES),
        cost_estimate=pl.CostEstimate(
            flops=2 * local * columns * (antennas * antennas + pairs * 2 * TILE_ANTENNAS**2),
            bytes_accessed=2 * local * (antennas * columns + pairs * 2 * TILE_ANTENNAS**2),
            transcendentals=0,
        ),
        name="correlate",
    )(order[:, None], ids[None, :], flags[None, :], *blocks)


def synthesize_kernel(beams_ref, proto_ref, table_ref, out_ref, zeta, planes):
    sources, _, local, columns = beams_ref.shape
    chans = sources * local
    spectra = columns // 2
    lane_tiles = chans // LANES
    words = 2 * lane_tiles
    out_frames = spectra - TAPS + 1
    group = planes.shape[0] // (out_frames * words)
    first_beam = pl.program_id(0) * group
    for member in range(group):
        rows = beams_ref[:, first_beam + member].reshape(chans, columns)
        for part in range(2):
            cols = slice(part * chans, (part + 1) * chans)
            value = None
            for source in range(2):
                term = lax.dot_general(
                    rows[:, source * spectra : (source + 1) * spectra],
                    table_ref[source * chans : (source + 1) * chans, cols],
                    (((0,), (0,)), ((), ())),
                    preferred_element_type=jnp.float32,
                )
                value = term if value is None else value + term
            value = value.astype(jnp.bfloat16).astype(jnp.float32)
            for tile in range(lane_tiles):
                lanes = slice(tile * LANES, (tile + 1) * LANES)
                zeta[...] = value[:, lanes]
                total = proto_ref[TAPS - 1 : TAPS, lanes] * zeta[pl.ds(0, out_frames), :]
                for tap in range(1, TAPS):
                    total = total + (
                        proto_ref[TAPS - 1 - tap : TAPS - tap, lanes]
                        * zeta[pl.ds(tap, out_frames), :]
                    )
                first = member * out_frames * words + 2 * tile + part
                planes[pl.ds(first, out_frames, stride=words), :] = total
    out_ref[...] = planes[...].astype(jnp.bfloat16)


def synthesize(arranged, proto, table):
    sources, beams, local, columns = arranged.shape
    chans = sources * local
    spectra = columns // 2
    lane_tiles = chans // LANES
    out_frames = spectra - TAPS + 1
    rows = out_frames * lane_tiles * 2
    group = 4 if beams % 4 == 0 else beams
    flat = pl.pallas_call(
        synthesize_kernel,
        grid=(beams // group,),
        in_specs=[
            pl.BlockSpec(memory_space=pltpu.VMEM),
            pl.BlockSpec((TAPS, chans), lambda b: (0, 0)),
            pl.BlockSpec((2 * chans, 2 * chans), lambda b: (0, 0)),
        ],
        out_specs=pl.BlockSpec((group * rows, LANES), lambda b: (b, 0)),
        out_shape=jax.ShapeDtypeStruct((beams * rows, LANES), jnp.bfloat16),
        scratch_shapes=[
            pltpu.VMEM((spectra, LANES), jnp.float32),
            pltpu.VMEM((group * rows, LANES), jnp.float32),
        ],
        compiler_params=pltpu.CompilerParams(vmem_limit_bytes=32 * 1024 * 1024),
        cost_estimate=pl.CostEstimate(
            flops=2 * beams * spectra * 4 * chans * chans,
            bytes_accessed=2 * beams * (columns + 2 * out_frames) * chans,
            transcendentals=0,
        ),
        name="synthesize",
    )(pltpu.with_memory_space_constraint(arranged, pltpu.VMEM), proto, table)
    return (
        flat.reshape(beams, out_frames, lane_tiles, 2, LANES)
        .transpose(0, 3, 1, 2, 4)
        .reshape(beams, 2, out_frames, chans)
    )


def turn(part):
    return lax.all_to_all(part, "chan", split_axis=0, concat_axis=0, tiled=True)


def exchange_early(first, second):
    devices = lax.axis_size("chan")
    me = lax.axis_index("chan")
    chans = first.shape[0]

    def send(source, mask):
        split = source.reshape((devices, chans // devices) + source.shape[1:])
        mine = lax.dynamic_index_in_dim(split, me ^ mask, 0, keepdims=False)
        if mask == 0:
            return mine
        return lax.ppermute(mine, "chan", [(i, i ^ mask) for i in range(devices)])

    far = [mask for mask in range(devices // 2, devices)]
    near = [mask for mask in range(devices // 2)]
    got = {mask: send(first, mask) for mask in far}
    late, second = lax.optimization_barrier((first, second))
    rest = turn(second)
    got.update({mask: send(late, mask) for mask in near})
    stacked = jnp.stack([got[mask] for mask in range(devices)])
    ordered = [
        lax.dynamic_index_in_dim(stacked, me ^ source, 0, keepdims=False)
        for source in range(devices)
    ]
    return jnp.concatenate(ordered, axis=0), rest


def per_device(samples, flags, delays, order):
    devices = lax.axis_size("chan")
    antennas_here, _, in_frames, chans = samples.shape
    local_channels = chans // devices
    spectra = in_frames - TAPS + 1
    antennas = antennas_here * devices
    beam_count = delays.shape[0]
    block = CHUNK_ANTENNAS if antennas_here > CHUNK_ANTENNAS else antennas_here
    sizes = [block, antennas_here - block] if antennas_here > block else [block]

    proto = jnp.asarray(prototype(TAPS, chans))
    table = jnp.asarray(transform_table(chans))

    parts = []
    columns_of = []
    start = 0
    for size in sizes:
        parts.append(channelize(samples, proto, table, start, size))
        ids = np.arange(antennas, dtype=np.int32).reshape(devices, antennas_here)
        columns_of.append(ids[:, start : start + size].reshape(-1))
        start += size
    ids = np.concatenate(columns_of)
    if len(parts) > 1:
        early, rest = exchange_early(parts[0], parts[1])
        parts = [early, rest]
    else:
        parts = [turn(parts[0])]
    blocks = [
        x.reshape(devices, local_channels, size, 2 * spectra) for x, size in zip(parts, sizes)
    ]

    def arrange(x):
        x = x.reshape(x.shape[:-1] + (devices, antennas_here))
        pieces = []
        at = 0
        for size in sizes:
            pieces.append(x[..., at : at + size].reshape(x.shape[:-2] + (devices * size,)))
            at += size
        return jnp.concatenate(pieces, axis=-1)

    flag_row = arrange(flags).astype(jnp.float32)
    keep = flag_row[None, :] * (1.0 / math.sqrt(antennas))
    weights = make_weights(
        arrange(delays), keep, lax.axis_index("chan") * local_channels, local_channels, chans
    )
    beams = form_beams(blocks, weights)
    arranged = turn(beams)
    arranged = arranged.reshape(devices, beam_count // devices, local_channels, 2 * spectra)
    visibilities = correlate(blocks, order, jnp.asarray(ids), flag_row)
    voltages = synthesize(arranged, proto, table)
    return visibilities, voltages


def solution(mesh):
    in_specs = (P(("groups", "chan"), None, None, None), P("groups"), P(), P("groups"))
    out_specs = (
        P(("groups", "chan"), None, None, None, None),
        P(("groups", "chan"), None, None, None),
    )

    return jax.shard_map(
        per_device, mesh=mesh, in_specs=in_specs, out_specs=out_specs, check_vma=False
    )
```

```python
import functools
import math

import jax
import jax.numpy as jnp
import ml_dtypes
import numpy as np
from jax import lax
from jax.experimental import pallas as pl
from jax.experimental.pallas import tpu as pltpu
from jax.sharding import PartitionSpec as P


TAPS = 16
TILE_ANTENNAS = 128
CHUNK_ANTENNAS = 16
FILTER_ANTENNAS = 8
LANES = 128
VMEM_BYTES = 60 * 1024 * 1024


def prototype(tap_count, chan_count):
    length = tap_count * chan_count
    counter = np.arange(length, dtype=np.float32)
    shifted = (counter - np.float32((length - 1) / 2.0)) / np.float32(chan_count)
    window = 0.5 - 0.5 * np.cos(2.0 * math.pi * (counter + 0.5) / length)
    return (np.sinc(shifted) * window).astype(np.float32).reshape(tap_count, chan_count)


def dft_parts(chan_count):
    counter = np.arange(chan_count)
    angle = (counter[:, None] * counter[None, :] % chan_count) * (2.0 * math.pi / chan_count)
    return np.cos(angle), np.sin(angle)


def round_bf16(table):
    return table.astype(np.float32).astype(ml_dtypes.bfloat16)


def transform_table(chan_count):
    cosine, sine = dft_parts(chan_count)
    table = np.concatenate(
        [np.concatenate([cosine, sine], axis=1), np.concatenate([-sine, cosine], axis=1)], axis=0
    )
    return (round_bf16(table).astype(np.float32) / math.sqrt(chan_count)).astype(
        ml_dtypes.bfloat16
    )


def channelize_kernel(me_ref, samples_ref, proto_ref, table_ref, *refs):
    out_refs, (planes, filtered, turned) = refs[:-3], refs[-3:]
    local, block, columns = out_refs[0].shape
    chans = local * len(out_refs)
    spectra = columns // 2
    lane_tiles = chans // LANES
    in_frames = spectra + TAPS - 1
    group = filtered.shape[1] // spectra
    words = 2 * lane_tiles
    rows = in_frames * words
    fold = block

    def convolve(step):
        planes[...] = samples_ref[step * group * rows : (step + 1) * group * rows, :].astype(jnp.float32)
        for member in range(group):
            for part in range(2):
                for tile in range(lane_tiles):
                    cols = slice(tile * LANES, (tile + 1) * LANES)
                    first = member * rows + 2 * tile + part
                    total = None
                    for tap in range(TAPS):
                        term = (
                            proto_ref[tap : tap + 1, cols]
                            * planes[pl.ds(first + tap * words, spectra, stride=words), :]
                        )
                        total = term if total is None else total + term
                    filtered[
                        step % 2,
                        member * spectra : (member + 1) * spectra,
                        part * chans + tile * LANES : part * chans + (tile + 1) * LANES,
                    ] = total.astype(jnp.bfloat16)

    def transform(step):
        product = lax.dot_general(
            table_ref[...],
            filtered[step % 2],
            (((1,), (1,)), ((), ())),
            preferred_element_type=jnp.float32,
        )
        for member in range(group):
            for part in range(2):
                ant = group * step + member
                turned[part, pl.ds(ant, chans, stride=fold), :] = product[
                    part * chans : (part + 1) * chans, member * spectra : (member + 1) * spectra
                ]

    steps = block // group
    convolve(0)
    for step in range(steps):
        if step + 1 < steps:
            convolve(step + 1)
        transform(step)
    for mask, out_ref in enumerate(out_refs):
        target = (me_ref[0] ^ mask) if len(out_refs) > 1 else 0
        here = pl.ds(pl.multiple_of(target * local * fold, local * fold), local * fold)
        for part in range(2):
            out_ref[:, :, part * spectra : (part + 1) * spectra] = (
                turned[part, here, :].reshape(local, fold, spectra).astype(jnp.bfloat16)
            )


def channelize(me, samples, proto, table, first, count, pieces):
    antennas, _, in_frames, chans = samples.shape
    spectra = in_frames - TAPS + 1
    lane_tiles = chans // LANES
    rows = in_frames * lane_tiles * 2
    block = FILTER_ANTENNAS if count % FILTER_ANTENNAS == 0 and first % FILTER_ANTENNAS == 0 else count
    group = block
    local = chans // pieces
    flat = (
        samples.reshape(antennas, 2, in_frames, lane_tiles, LANES)
        .transpose(0, 2, 3, 1, 4)
        .reshape(antennas * rows, LANES)
    )
    return pl.pallas_call(
        channelize_kernel,
        grid=(count // block,),
        in_specs=[
            pl.BlockSpec(memory_space=pltpu.SMEM),
            pl.BlockSpec((block * rows, LANES), lambda i: (i + first // block, 0)),
            pl.BlockSpec((TAPS, chans), lambda i: (0, 0)),
            pl.BlockSpec((2 * chans, 2 * chans), lambda i: (0, 0)),
        ],
        out_specs=[pl.BlockSpec((local, block, 2 * spectra), lambda i: (0, i, 0))] * pieces,
        out_shape=[jax.ShapeDtypeStruct((local, count, 2 * spectra), jnp.bfloat16)] * pieces,
        scratch_shapes=[
            pltpu.VMEM((group * rows, LANES), jnp.float32),
            pltpu.VMEM((2, group * spectra, 2 * chans), jnp.bfloat16),
            pltpu.VMEM((2, chans * block, spectra), jnp.float32),
        ],
        compiler_params=pltpu.CompilerParams(vmem_limit_bytes=VMEM_BYTES),
        cost_estimate=pl.CostEstimate(
            flops=count * spectra * 4 * chans * 2 * chans * 2,
            bytes_accessed=count * 2 * (in_frames + spectra) * chans * 2,
            transcendentals=0,
        ),
        name="channelize",
    )(me.reshape(1), flat, proto, table)


def weights_kernel(start_cos, start_sin, turn_cos, turn_sin, keep_ref, out_ref, cosine, sine):
    local, double_beams, _ = out_ref.shape
    beams = double_beams // 2
    rows = 8 if beams % 8 == 0 else beams
    cosine[...] = start_cos[...]
    sine[...] = start_sin[...]

    def channel(c, carry):
        def strip(i, inner):
            here = pl.ds(pl.multiple_of(i * 2 * rows, 2 * rows), 2 * rows)
            there = pl.ds(pl.multiple_of(i * 2 * rows + beams, 2 * rows), 2 * rows)
            co, si = cosine[here, :], sine[here, :]
            tc, ts = turn_cos[here, :], turn_sin[here, :]
            out_ref[c, here, :] = (co * keep_ref[...]).astype(jnp.bfloat16)
            out_ref[c, there, :] = (si * keep_ref[...]).astype(jnp.bfloat16)
            cosine[here, :] = co * tc - si * ts
            sine[here, :] = si * tc + co * ts
            return inner

        return lax.fori_loop(0, beams // (2 * rows), strip, carry)

    lax.fori_loop(0, local, channel, 0)


def make_weights(delays, keep, first_channel, local, chans):
    beams, antennas = delays.shape
    step = 2.0 * math.pi / chans
    start = (delays * first_channel % chans).astype(jnp.float32) * step
    turns = delays.astype(jnp.float32) * step
    vmem = pl.BlockSpec(memory_space=pltpu.VMEM)
    return pl.pallas_call(
        weights_kernel,
        in_specs=[vmem] * 5,
        out_specs=vmem,
        out_shape=jax.ShapeDtypeStruct((local, 2 * beams, antennas), jnp.bfloat16),
        scratch_shapes=[pltpu.VMEM((beams, antennas), jnp.float32)] * 2,
        compiler_params=pltpu.CompilerParams(vmem_limit_bytes=40 * 1024 * 1024),
        cost_estimate=pl.CostEstimate(
            flops=10 * local * beams * antennas,
            bytes_accessed=4 * 4 * beams * antennas + 4 * local * beams * antennas,
            transcendentals=0,
        ),
        name="make_weights",
    )(jnp.cos(start), jnp.sin(start), jnp.cos(turns), jnp.sin(turns), keep)


def beam_kernel(counts, *refs):
    kinds = len(counts) + 1
    sources, (out_ref, turned), holds, sems = (
        refs[:kinds], refs[kinds : kinds + 2], refs[kinds + 2 : -1], refs[-1]
    )
    beams, local, columns = out_ref.shape
    spectra = columns // 2

    def copies(channel):
        views = [x.at[:, channel] for x in sources[:-1]] + [sources[-1].at[channel]]
        return [
            pltpu.make_async_copy(view, hold.at[channel], sems.at[kind, channel])
            for kind, (view, hold) in enumerate(zip(views, holds))
        ]

    def begin(channel, carry):
        for copy in copies(channel):
            copy.start()
        return carry

    lax.fori_loop(0, local, begin, 0)

    def form(channel, carry):
        for copy in copies(channel):
            copy.wait()
        product = None
        start = 0
        for hold, count in zip(holds, counts):
            term = jnp.dot(
                holds[-1][channel, :, start : start + count],
                hold[channel].reshape(count, columns),
                preferred_element_type=jnp.float32,
            )
            product = term if product is None else product + term
            start += count
        rows = pl.ds(channel, beams, stride=local)
        turned[0, rows, :] = product[:beams, :spectra] + product[beams:, spectra:]
        turned[1, rows, :] = product[:beams, spectra:] - product[beams:, :spectra]
        return carry

    lax.fori_loop(0, local, form, 0)
    for part in range(2):
        out_ref[:, :, part * spectra : (part + 1) * spectra] = (
            turned[part].reshape(beams, local, spectra).astype(jnp.bfloat16)
        )


def form_beams(blocks, weights):
    local, double_beams, antennas = weights.shape
    beams = double_beams // 2
    columns = blocks[0].shape[3]
    counts = tuple(x.shape[0] * x.shape[2] for x in blocks)
    return pl.pallas_call(
        functools.partial(beam_kernel, counts),
        in_specs=[pl.BlockSpec(memory_space=pl.ANY)] * (len(blocks) + 1),
        out_specs=pl.BlockSpec(memory_space=pltpu.VMEM),
        out_shape=jax.ShapeDtypeStruct((beams, local, columns), jnp.bfloat16),
        scratch_shapes=[pltpu.VMEM((2, beams * local, columns // 2), jnp.float32)]
        + [pltpu.VMEM((local, x.shape[0], x.shape[2], columns), jnp.bfloat16) for x in blocks]
        + [
            pltpu.VMEM((local, double_beams, antennas), jnp.bfloat16),
            pltpu.SemaphoreType.DMA((len(blocks) + 1, local)),
        ],
        compiler_params=pltpu.CompilerParams(vmem_limit_bytes=VMEM_BYTES),
        cost_estimate=pl.CostEstimate(
            flops=2 * local * double_beams * antennas * columns,
            bytes_accessed=2 * local * (double_beams * antennas + antennas * columns + beams * columns),
            transcendentals=0,
        ),
        name="form_beams",
    )(*blocks, weights)


def visibility_kernel(counts, order_ref, ids_ref, flags_ref, *refs):
    x_refs = refs[: len(counts)]
    out_ref, select, permuted, turned = refs[len(counts) :]
    antennas, columns = permuted.shape
    spectra = columns // 2
    tile = TILE_ANTENNAS
    tiles = antennas // tile

    @pl.when(pl.program_id(0) == 0)
    def _():
        def fill(t, carry):
            rows = pl.ds(pl.multiple_of(t * tile, tile), tile)
            select[rows, :] = jnp.where(
                order_ref[rows, :] == ids_ref[...], flags_ref[...], 0.0
            ).astype(jnp.bfloat16)
            return carry

        lax.fori_loop(0, tiles, fill, 0)

    product = None
    start = 0
    for x_ref, count in zip(x_refs, counts):
        term = jnp.dot(
            select[:, start : start + count],
            x_ref[:, 0].reshape(count, columns),
            preferred_element_type=jnp.float32,
        )
        product = term if product is None else product + term
        start += count
    permuted[...] = product.astype(jnp.bfloat16)
    scaled = product * (1.0 / spectra)
    for t in range(tiles):
        block = scaled[t * tile : (t + 1) * tile, :]
        turned[2 * t * tile : (2 * t + 1) * tile, :] = block.astype(jnp.bfloat16)
        turned[(2 * t + 1) * tile : (2 * t + 2) * tile, :spectra] = block[:, spectra:].astype(jnp.bfloat16)
        turned[(2 * t + 1) * tile : (2 * t + 2) * tile, spectra:] = (-block[:, :spectra]).astype(jnp.bfloat16)
    pair = 0
    for p in range(tiles):
        left = turned[2 * p * tile : (2 * p + 2) * tile, :]
        result = lax.dot_general(
            left,
            permuted[p * tile :, :],
            (((1,), (1,)), ((), ())),
            preferred_element_type=jnp.float32,
        ).astype(jnp.bfloat16)
        for q in range(p, tiles):
            cols = slice((q - p) * tile, (q - p + 1) * tile)
            out_ref[0, pair, 0] = result[:tile, cols]
            out_ref[0, pair, 1] = result[tile:, cols]
            pair += 1


def correlate(blocks, order, ids, flags):
    antennas = order.shape[0]
    local, columns = blocks[0].shape[1], blocks[0].shape[3]
    counts = tuple(x.shape[0] * x.shape[2] for x in blocks)
    tiles = antennas // TILE_ANTENNAS
    pairs = tiles * (tiles + 1) // 2
    return pl.pallas_call(
        functools.partial(visibility_kernel, counts),
        grid=(local,),
        in_specs=[
            pl.BlockSpec((antennas, 1), lambda c: (0, 0)),
            pl.BlockSpec((1, antennas), lambda c: (0, 0)),
            pl.BlockSpec((1, antennas), lambda c: (0, 0)),
        ]
        + [
            pl.BlockSpec((x.shape[0], 1, x.shape[2], columns), lambda c: (0, c, 0, 0))
            for x in blocks
        ],
        out_specs=pl.BlockSpec(
            (1, pairs, 2, TILE_ANTENNAS, TILE_ANTENNAS), lambda c: (c, 0, 0, 0, 0)
        ),
        out_shape=jax.ShapeDtypeStruct(
            (local, pairs, 2, TILE_ANTENNAS, TILE_ANTENNAS), jnp.bfloat16
        ),
        scratch_shapes=[
            pltpu.VMEM((antennas, antennas), jnp.bfloat16),
            pltpu.VMEM((antennas, columns), jnp.bfloat16),
            pltpu.VMEM((2 * antennas, columns), jnp.bfloat16),
        ],
        compiler_params=pltpu.CompilerParams(vmem_limit_bytes=VMEM_BYTES),
        cost_estimate=pl.CostEstimate(
            flops=2 * local * columns * (antennas * antennas + pairs * 2 * TILE_ANTENNAS**2),
            bytes_accessed=2 * local * (antennas * columns + pairs * 2 * TILE_ANTENNAS**2),
            transcendentals=0,
        ),
        name="correlate",
    )(order[:, None], ids[None, :], flags[None, :], *blocks)


def synthesize_kernel(beams_ref, proto_ref, table_ref, out_ref, zeta, planes):
    sources, _, local, columns = beams_ref.shape
    chans = sources * local
    spectra = columns // 2
    lane_tiles = chans // LANES
    words = 2 * lane_tiles
    out_frames = spectra - TAPS + 1
    group = planes.shape[0] // (out_frames * words)
    first_beam = pl.program_id(0) * group
    for member in range(group):
        rows = beams_ref[:, first_beam + member].reshape(chans, columns)
        for part in range(2):
            cols = slice(part * chans, (part + 1) * chans)
            value = None
            for source in range(2):
                term = lax.dot_general(
                    rows[:, source * spectra : (source + 1) * spectra],
                    table_ref[source * chans : (source + 1) * chans, cols],
                    (((0,), (0,)), ((), ())),
                    preferred_element_type=jnp.float32,
                )
                value = term if value is None else value + term
            value = value.astype(jnp.bfloat16).astype(jnp.float32)
            for tile in range(lane_tiles):
                lanes = slice(tile * LANES, (tile + 1) * LANES)
                zeta[...] = value[:, lanes]
                total = proto_ref[TAPS - 1 : TAPS, lanes] * zeta[pl.ds(0, out_frames), :]
                for tap in range(1, TAPS):
                    total = total + (
                        proto_ref[TAPS - 1 - tap : TAPS - tap, lanes]
                        * zeta[pl.ds(tap, out_frames), :]
                    )
                first = member * out_frames * words + 2 * tile + part
                planes[pl.ds(first, out_frames, stride=words), :] = total
    out_ref[...] = planes[...].astype(jnp.bfloat16)


def synthesize(arranged, proto, table):
    sources, beams, local, columns = arranged.shape
    chans = sources * local
    spectra = columns // 2
    lane_tiles = chans // LANES
    out_frames = spectra - TAPS + 1
    rows = out_frames * lane_tiles * 2
    group = 4 if beams % 4 == 0 else beams
    flat = pl.pallas_call(
        synthesize_kernel,
        grid=(beams // group,),
        in_specs=[
            pl.BlockSpec(memory_space=pltpu.VMEM),
            pl.BlockSpec((TAPS, chans), lambda b: (0, 0)),
            pl.BlockSpec((2 * chans, 2 * chans), lambda b: (0, 0)),
        ],
        out_specs=pl.BlockSpec((group * rows, LANES), lambda b: (b, 0)),
        out_shape=jax.ShapeDtypeStruct((beams * rows, LANES), jnp.bfloat16),
        scratch_shapes=[
            pltpu.VMEM((spectra, LANES), jnp.float32),
            pltpu.VMEM((group * rows, LANES), jnp.float32),
        ],
        compiler_params=pltpu.CompilerParams(vmem_limit_bytes=32 * 1024 * 1024),
        cost_estimate=pl.CostEstimate(
            flops=2 * beams * spectra * 4 * chans * chans,
            bytes_accessed=2 * beams * (columns + 2 * out_frames) * chans,
            transcendentals=0,
        ),
        name="synthesize",
    )(pltpu.with_memory_space_constraint(arranged, pltpu.VMEM), proto, table)
    return (
        flat.reshape(beams, out_frames, lane_tiles, 2, LANES)
        .transpose(0, 3, 1, 2, 4)
        .reshape(beams, 2, out_frames, chans)
    )


def turn(part):
    return lax.all_to_all(part, "chan", split_axis=0, concat_axis=0, tiled=True)


def exchange_early(pieces, second):
    devices = lax.axis_size("chan")
    me = lax.axis_index("chan")

    def send(piece, mask):
        return lax.ppermute(piece, "chan", [(i, i ^ mask) for i in range(devices)])

    half = devices // 2
    far = [send(pieces[mask], mask) for mask in range(half, devices)]
    late, second = lax.optimization_barrier((pieces[:half], second))
    rest = turn(second)
    near = [late[0]] + [send(late[mask], mask) for mask in range(1, half)]
    stacked = jnp.stack(near + far)
    ordered = [
        lax.dynamic_index_in_dim(stacked, me ^ source, 0, keepdims=False)
        for source in range(devices)
    ]
    return [jnp.concatenate(ordered, axis=0), rest]


def per_device(samples, flags, delays, order):
    devices = lax.axis_size("chan")
    antennas_here, _, in_frames, chans = samples.shape
    local_channels = chans // devices
    spectra = in_frames - TAPS + 1
    antennas = antennas_here * devices
    beam_count = delays.shape[0]
    block = CHUNK_ANTENNAS if antennas_here > CHUNK_ANTENNAS else antennas_here
    paired = devices & (devices - 1) == 0 and antennas_here > block
    sizes = [block, antennas_here - block] if paired else [antennas_here]

    proto = jnp.asarray(prototype(TAPS, chans))
    table = jnp.asarray(transform_table(chans))

    me = lax.axis_index("chan")
    parts = []
    columns_of = []
    start = 0
    for size in sizes:
        pieces = devices if len(sizes) > 1 and start == 0 else 1
        parts.append(channelize(me, samples, proto, table, start, size, pieces))
        ids = np.arange(antennas, dtype=np.int32).reshape(devices, antennas_here)
        columns_of.append(ids[:, start : start + size].reshape(-1))
        start += size
    ids = np.concatenate(columns_of)
    if len(parts) > 1:
        parts = exchange_early(parts[0], parts[1][0])
    else:
        parts = [turn(parts[0][0])]
    blocks = [
        x.reshape(devices, local_channels, size, 2 * spectra) for x, size in zip(parts, sizes)
    ]

    def arrange(x):
        x = x.reshape(x.shape[:-1] + (devices, antennas_here))
        pieces = []
        at = 0
        for size in sizes:
            pieces.append(x[..., at : at + size].reshape(x.shape[:-2] + (devices * size,)))
            at += size
        return jnp.concatenate(pieces, axis=-1)

    flag_row = arrange(flags).astype(jnp.float32)
    keep = flag_row[None, :] * (1.0 / math.sqrt(antennas))
    weights = make_weights(
        arrange(delays), keep, lax.axis_index("chan") * local_channels, local_channels, chans
    )
    beams = form_beams(blocks, weights)
    arranged = turn(beams)
    arranged = arranged.reshape(devices, beam_count // devices, local_channels, 2 * spectra)
    visibilities = correlate(blocks, order, jnp.asarray(ids), flag_row)
    voltages = synthesize(arranged, proto, table)
    return visibilities, voltages


def solution(mesh):
    in_specs = (P(("groups", "chan"), None, None, None), P("groups"), P(), P("groups"))
    out_specs = (
        P(("groups", "chan"), None, None, None, None),
        P(("groups", "chan"), None, None, None),
    )

    return jax.shard_map(
        per_device, mesh=mesh, in_specs=in_specs, out_specs=out_specs, check_vma=False
    )
```

```python
import functools
import math

import jax
import jax.numpy as jnp
import ml_dtypes
import numpy as np
from jax import lax
from jax.experimental import pallas as pl
from jax.experimental.pallas import tpu as pltpu
from jax.sharding import PartitionSpec as P


TAPS = 16
TILE_ANTENNAS = 128
CHUNK_ANTENNAS = 16
FILTER_ANTENNAS = 8
LANES = 128
VMEM_BYTES = 60 * 1024 * 1024


def prototype(tap_count, chan_count):
    length = tap_count * chan_count
    counter = np.arange(length, dtype=np.float32)
    shifted = (counter - np.float32((length - 1) / 2.0)) / np.float32(chan_count)
    window = 0.5 - 0.5 * np.cos(2.0 * math.pi * (counter + 0.5) / length)
    return (np.sinc(shifted) * window).astype(np.float32).reshape(tap_count, chan_count)


def dft_parts(chan_count):
    counter = np.arange(chan_count)
    angle = (counter[:, None] * counter[None, :] % chan_count) * (2.0 * math.pi / chan_count)
    return np.cos(angle), np.sin(angle)


def round_bf16(table):
    return table.astype(np.float32).astype(ml_dtypes.bfloat16)


def transform_table(chan_count):
    cosine, sine = dft_parts(chan_count)
    table = np.concatenate(
        [np.concatenate([cosine, sine], axis=1), np.concatenate([-sine, cosine], axis=1)], axis=0
    )
    return (round_bf16(table).astype(np.float32) / math.sqrt(chan_count)).astype(
        ml_dtypes.bfloat16
    )


def channelize_kernel(me_ref, samples_ref, proto_ref, table_ref, *refs):
    out_refs, (planes, filtered, turned) = refs[:-3], refs[-3:]
    local, block, columns = out_refs[0].shape
    chans = local * len(out_refs)
    spectra = columns // 2
    lane_tiles = chans // LANES
    in_frames = spectra + TAPS - 1
    group = filtered.shape[1] // spectra
    words = 2 * lane_tiles
    rows = in_frames * words
    fold = block

    def convolve(step):
        planes[...] = samples_ref[step * group * rows : (step + 1) * group * rows, :].astype(jnp.float32)
        for member in range(group):
            for part in range(2):
                for tile in range(lane_tiles):
                    cols = slice(tile * LANES, (tile + 1) * LANES)
                    first = member * rows + 2 * tile + part
                    total = None
                    for tap in range(TAPS):
                        term = (
                            proto_ref[tap : tap + 1, cols]
                            * planes[pl.ds(first + tap * words, spectra, stride=words), :]
                        )
                        total = term if total is None else total + term
                    filtered[
                        step % 2,
                        member * spectra : (member + 1) * spectra,
                        part * chans + tile * LANES : part * chans + (tile + 1) * LANES,
                    ] = total.astype(jnp.bfloat16)

    def transform(step):
        product = lax.dot_general(
            table_ref[...],
            filtered[step % 2],
            (((1,), (1,)), ((), ())),
            preferred_element_type=jnp.float32,
        )
        for member in range(group):
            for part in range(2):
                ant = group * step + member
                turned[part, pl.ds(ant, chans, stride=fold), :] = product[
                    part * chans : (part + 1) * chans, member * spectra : (member + 1) * spectra
                ]

    steps = block // group
    convolve(0)
    for step in range(steps):
        if step + 1 < steps:
            convolve(step + 1)
        transform(step)
    for mask, out_ref in enumerate(out_refs):
        target = (me_ref[0] ^ mask) if len(out_refs) > 1 else 0
        here = pl.ds(pl.multiple_of(target * local * fold, local * fold), local * fold)
        for part in range(2):
            out_ref[:, :, part * spectra : (part + 1) * spectra] = (
                turned[part, here, :].reshape(local, fold, spectra).astype(jnp.bfloat16)
            )


def channelize(me, samples, proto, table, first, count, pieces):
    antennas, _, in_frames, chans = samples.shape
    spectra = in_frames - TAPS + 1
    lane_tiles = chans // LANES
    rows = in_frames * lane_tiles * 2
    block = FILTER_ANTENNAS if count % FILTER_ANTENNAS == 0 and first % FILTER_ANTENNAS == 0 else count
    group = block
    local = chans // pieces
    flat = (
        samples.reshape(antennas, 2, in_frames, lane_tiles, LANES)
        .transpose(0, 2, 3, 1, 4)
        .reshape(antennas * rows, LANES)
    )
    return pl.pallas_call(
        channelize_kernel,
        grid=(count // block,),
        in_specs=[
            pl.BlockSpec(memory_space=pltpu.SMEM),
            pl.BlockSpec((block * rows, LANES), lambda i: (i + first // block, 0)),
            pl.BlockSpec((TAPS, chans), lambda i: (0, 0)),
            pl.BlockSpec((2 * chans, 2 * chans), lambda i: (0, 0)),
        ],
        out_specs=[pl.BlockSpec((local, block, 2 * spectra), lambda i: (0, i, 0))] * pieces,
        out_shape=[jax.ShapeDtypeStruct((local, count, 2 * spectra), jnp.bfloat16)] * pieces,
        scratch_shapes=[
            pltpu.VMEM((group * rows, LANES), jnp.float32),
            pltpu.VMEM((2, group * spectra, 2 * chans), jnp.bfloat16),
            pltpu.VMEM((2, chans * block, spectra), jnp.float32),
        ],
        compiler_params=pltpu.CompilerParams(vmem_limit_bytes=VMEM_BYTES),
        cost_estimate=pl.CostEstimate(
            flops=count * spectra * 4 * chans * 2 * chans * 2,
            bytes_accessed=count * 2 * (in_frames + spectra) * chans * 2,
            transcendentals=0,
        ),
        name="channelize",
    )(me.reshape(1), flat, proto, table)


def weights_kernel(start_cos, start_sin, turn_cos, turn_sin, keep_ref, out_ref, cosine, sine):
    local, double_beams, _ = out_ref.shape
    beams = double_beams // 2
    rows = 8 if beams % 8 == 0 else beams
    cosine[...] = start_cos[...]
    sine[...] = start_sin[...]

    def channel(c, carry):
        def strip(i, inner):
            here = pl.ds(pl.multiple_of(i * 2 * rows, 2 * rows), 2 * rows)
            there = pl.ds(pl.multiple_of(i * 2 * rows + beams, 2 * rows), 2 * rows)
            co, si = cosine[here, :], sine[here, :]
            tc, ts = turn_cos[here, :], turn_sin[here, :]
            out_ref[c, here, :] = (co * keep_ref[...]).astype(jnp.bfloat16)
            out_ref[c, there, :] = (si * keep_ref[...]).astype(jnp.bfloat16)
            cosine[here, :] = co * tc - si * ts
            sine[here, :] = si * tc + co * ts
            return inner

        return lax.fori_loop(0, beams // (2 * rows), strip, carry)

    lax.fori_loop(0, local, channel, 0)


def make_weights(delays, keep, first_channel, local, chans):
    beams, antennas = delays.shape
    step = 2.0 * math.pi / chans
    start = (delays * first_channel % chans).astype(jnp.float32) * step
    turns = delays.astype(jnp.float32) * step
    vmem = pl.BlockSpec(memory_space=pltpu.VMEM)
    return pl.pallas_call(
        weights_kernel,
        in_specs=[vmem] * 5,
        out_specs=vmem,
        out_shape=jax.ShapeDtypeStruct((local, 2 * beams, antennas), jnp.bfloat16),
        scratch_shapes=[pltpu.VMEM((beams, antennas), jnp.float32)] * 2,
        compiler_params=pltpu.CompilerParams(vmem_limit_bytes=40 * 1024 * 1024),
        cost_estimate=pl.CostEstimate(
            flops=10 * local * beams * antennas,
            bytes_accessed=4 * 4 * beams * antennas + 4 * local * beams * antennas,
            transcendentals=0,
        ),
        name="make_weights",
    )(jnp.cos(start), jnp.sin(start), jnp.cos(turns), jnp.sin(turns), keep)


def beam_kernel(counts, *refs):
    kinds = len(counts) + 1
    sources, (out_ref, turned, rounded), holds, (sems, out_sems) = (
        refs[:kinds], refs[kinds : kinds + 3], refs[kinds + 3 : -2], refs[-2:]
    )
    beams, local, columns = out_ref.shape
    spectra = columns // 2

    def copies(channel):
        views = [x.at[:, channel] for x in sources[:-1]] + [sources[-1].at[channel]]
        return [
            pltpu.make_async_copy(view, hold.at[channel], sems.at[kind, channel])
            for kind, (view, hold) in enumerate(zip(views, holds))
        ]

    def begin(channel, carry):
        for copy in copies(channel):
            copy.start()
        return carry

    lax.fori_loop(0, local, begin, 0)

    def form(channel, carry):
        for copy in copies(channel):
            copy.wait()
        product = None
        start = 0
        for hold, count in zip(holds, counts):
            term = jnp.dot(
                holds[-1][channel, :, start : start + count],
                hold[channel].reshape(count, columns),
                preferred_element_type=jnp.float32,
            )
            product = term if product is None else product + term
            start += count
        rows = pl.ds(channel, beams, stride=local)
        turned[0, rows, :] = product[:beams, :spectra] + product[beams:, spectra:]
        turned[1, rows, :] = product[:beams, spectra:] - product[beams:, :spectra]
        return carry

    lax.fori_loop(0, local, form, 0)
    slices = rounded.shape[0]
    count = beams // slices
    writes = []
    for i in range(slices):
        for part in range(2):
            rounded[i, :, :, part * spectra : (part + 1) * spectra] = (
                turned[part, i * count * local : (i + 1) * count * local, :]
                .reshape(count, local, spectra)
                .astype(jnp.bfloat16)
            )
        write = pltpu.make_async_copy(
            rounded.at[i], out_ref.at[i * count : (i + 1) * count], out_sems.at[i]
        )
        write.start()
        writes.append(write)
    for write in writes:
        write.wait()


def form_beams(blocks, weights):
    local, double_beams, antennas = weights.shape
    beams = double_beams // 2
    columns = blocks[0].shape[3]
    counts = tuple(x.shape[0] * x.shape[2] for x in blocks)
    slices = 4 if beams % 4 == 0 else 1
    return pl.pallas_call(
        functools.partial(beam_kernel, counts),
        in_specs=[pl.BlockSpec(memory_space=pl.ANY)] * (len(blocks) + 1),
        out_specs=pl.BlockSpec(memory_space=pl.ANY),
        out_shape=jax.ShapeDtypeStruct((beams, local, columns), jnp.bfloat16),
        scratch_shapes=[
            pltpu.VMEM((2, beams * local, columns // 2), jnp.float32),
            pltpu.VMEM((slices, beams // slices, local, columns), jnp.bfloat16),
        ]
        + [pltpu.VMEM((local, x.shape[0], x.shape[2], columns), jnp.bfloat16) for x in blocks]
        + [
            pltpu.VMEM((local, double_beams, antennas), jnp.bfloat16),
            pltpu.SemaphoreType.DMA((len(blocks) + 1, local)),
            pltpu.SemaphoreType.DMA((slices,)),
        ],
        compiler_params=pltpu.CompilerParams(vmem_limit_bytes=VMEM_BYTES),
        cost_estimate=pl.CostEstimate(
            flops=2 * local * double_beams * antennas * columns,
            bytes_accessed=2 * local * (double_beams * antennas + antennas * columns + beams * columns),
            transcendentals=0,
        ),
        name="form_beams",
    )(*blocks, weights)


def visibility_kernel(counts, order_ref, ids_ref, flags_ref, *refs):
    x_refs = refs[: len(counts)]
    out_ref, select, permuted, turned = refs[len(counts) :]
    antennas, columns = permuted.shape
    spectra = columns // 2
    tile = TILE_ANTENNAS
    tiles = antennas // tile

    @pl.when(pl.program_id(0) == 0)
    def _():
        def fill(t, carry):
            rows = pl.ds(pl.multiple_of(t * tile, tile), tile)
            select[rows, :] = jnp.where(
                order_ref[rows, :] == ids_ref[...], flags_ref[...], 0.0
            ).astype(jnp.bfloat16)
            return carry

        lax.fori_loop(0, tiles, fill, 0)

    product = None
    start = 0
    for x_ref, count in zip(x_refs, counts):
        term = jnp.dot(
            select[:, start : start + count],
            x_ref[:, 0].reshape(count, columns),
            preferred_element_type=jnp.float32,
        )
        product = term if product is None else product + term
        start += count
    permuted[...] = product.astype(jnp.bfloat16)
    scaled = product * (1.0 / spectra)
    for t in range(tiles):
        block = scaled[t * tile : (t + 1) * tile, :]
        turned[2 * t * tile : (2 * t + 1) * tile, :] = block.astype(jnp.bfloat16)
        turned[(2 * t + 1) * tile : (2 * t + 2) * tile, :spectra] = block[:, spectra:].astype(jnp.bfloat16)
        turned[(2 * t + 1) * tile : (2 * t + 2) * tile, spectra:] = (-block[:, :spectra]).astype(jnp.bfloat16)
    pair = 0
    for p in range(tiles):
        left = turned[2 * p * tile : (2 * p + 2) * tile, :]
        result = lax.dot_general(
            left,
            permuted[p * tile :, :],
            (((1,), (1,)), ((), ())),
            preferred_element_type=jnp.float32,
        ).astype(jnp.bfloat16)
        for q in range(p, tiles):
            cols = slice((q - p) * tile, (q - p + 1) * tile)
            out_ref[0, pair, 0] = result[:tile, cols]
            out_ref[0, pair, 1] = result[tile:, cols]
            pair += 1


def correlate(blocks, order, ids, flags):
    antennas = order.shape[0]
    local, columns = blocks[0].shape[1], blocks[0].shape[3]
    counts = tuple(x.shape[0] * x.shape[2] for x in blocks)
    tiles = antennas // TILE_ANTENNAS
    pairs = tiles * (tiles + 1) // 2
    return pl.pallas_call(
        functools.partial(visibility_kernel, counts),
        grid=(local,),
        in_specs=[
            pl.BlockSpec((antennas, 1), lambda c: (0, 0)),
            pl.BlockSpec((1, antennas), lambda c: (0, 0)),
            pl.BlockSpec((1, antennas), lambda c: (0, 0)),
        ]
        + [
            pl.BlockSpec((x.shape[0], 1, x.shape[2], columns), lambda c: (0, c, 0, 0))
            for x in blocks
        ],
        out_specs=pl.BlockSpec(
            (1, pairs, 2, TILE_ANTENNAS, TILE_ANTENNAS), lambda c: (c, 0, 0, 0, 0)
        ),
        out_shape=jax.ShapeDtypeStruct(
            (local, pairs, 2, TILE_ANTENNAS, TILE_ANTENNAS), jnp.bfloat16
        ),
        scratch_shapes=[
            pltpu.VMEM((antennas, antennas), jnp.bfloat16),
            pltpu.VMEM((antennas, columns), jnp.bfloat16),
            pltpu.VMEM((2 * antennas, columns), jnp.bfloat16),
        ],
        compiler_params=pltpu.CompilerParams(vmem_limit_bytes=VMEM_BYTES),
        cost_estimate=pl.CostEstimate(
            flops=2 * local * columns * (antennas * antennas + pairs * 2 * TILE_ANTENNAS**2),
            bytes_accessed=2 * local * (antennas * columns + pairs * 2 * TILE_ANTENNAS**2),
            transcendentals=0,
        ),
        name="correlate",
    )(order[:, None], ids[None, :], flags[None, :], *blocks)


def synthesize_kernel(beams_ref, proto_ref, table_ref, out_ref, zeta, planes):
    sources, _, local, columns = beams_ref.shape
    chans = sources * local
    spectra = columns // 2
    lane_tiles = chans // LANES
    words = 2 * lane_tiles
    out_frames = spectra - TAPS + 1
    group = planes.shape[0] // (out_frames * words)
    first_beam = pl.program_id(0) * group
    for member in range(group):
        rows = beams_ref[:, first_beam + member].reshape(chans, columns)
        left = jnp.concatenate([rows[:, :spectra].T, rows[:, spectra:].T], axis=1)
        both = jnp.dot(left, table_ref[...], preferred_element_type=jnp.float32)
        for part in range(2):
            value = both[:, part * chans : (part + 1) * chans]
            value = value.astype(jnp.bfloat16).astype(jnp.float32)
            for tile in range(lane_tiles):
                lanes = slice(tile * LANES, (tile + 1) * LANES)
                slot = (member * 2 + part) * lane_tiles + tile
                zeta[slot, 0:spectra, :] = value[:, lanes]
                total = proto_ref[TAPS - 1 : TAPS, lanes] * zeta[slot, pl.ds(0, out_frames), :]
                for tap in range(1, TAPS):
                    total = total + (
                        proto_ref[TAPS - 1 - tap : TAPS - tap, lanes]
                        * zeta[slot, pl.ds(tap, out_frames), :]
                    )
                first = member * out_frames * words + 2 * tile + part
                planes[pl.ds(first, out_frames, stride=words), :] = total
    out_ref[...] = planes[0 : out_ref.shape[0], :].astype(jnp.bfloat16)


def synthesize(arranged, proto, table):
    sources, beams, local, columns = arranged.shape
    chans = sources * local
    spectra = columns // 2
    lane_tiles = chans // LANES
    out_frames = spectra - TAPS + 1
    rows = out_frames * lane_tiles * 2
    group = 4 if beams % 4 == 0 else beams
    flat = pl.pallas_call(
        synthesize_kernel,
        grid=(beams // group,),
        in_specs=[
            pl.BlockSpec(memory_space=pltpu.VMEM),
            pl.BlockSpec((TAPS, chans), lambda b: (0, 0)),
            pl.BlockSpec((2 * chans, 2 * chans), lambda b: (0, 0)),
        ],
        out_specs=pl.BlockSpec((group * rows, LANES), lambda b: (b, 0)),
        out_shape=jax.ShapeDtypeStruct((beams * rows, LANES), jnp.bfloat16),
        scratch_shapes=[
            pltpu.VMEM((group * 2 * lane_tiles, spectra + 8, LANES), jnp.float32),
            pltpu.VMEM((group * rows + 16 * lane_tiles, LANES), jnp.float32),
        ],
        compiler_params=pltpu.CompilerParams(vmem_limit_bytes=32 * 1024 * 1024),
        cost_estimate=pl.CostEstimate(
            flops=2 * beams * spectra * 4 * chans * chans,
            bytes_accessed=2 * beams * (columns + 2 * out_frames) * chans,
            transcendentals=0,
        ),
        name="synthesize",
    )(pltpu.with_memory_space_constraint(arranged, pltpu.VMEM), proto, table)
    return (
        flat.reshape(beams, out_frames, lane_tiles, 2, LANES)
        .transpose(0, 3, 1, 2, 4)
        .reshape(beams, 2, out_frames, chans)
    )


def turn(part):
    return lax.all_to_all(part, "chan", split_axis=0, concat_axis=0, tiled=True)


def exchange_early(pieces, second):
    devices = lax.axis_size("chan")
    me = lax.axis_index("chan")

    def send(piece, mask):
        return lax.ppermute(piece, "chan", [(i, i ^ mask) for i in range(devices)])

    half = devices // 2
    far = [send(pieces[mask], mask) for mask in range(half, devices)]
    late, second = lax.optimization_barrier((pieces[:half], second))
    rest = turn(second)
    near = [late[0]] + [send(late[mask], mask) for mask in range(1, half)]
    stacked = jnp.stack(near + far)
    ordered = [
        lax.dynamic_index_in_dim(stacked, me ^ source, 0, keepdims=False)
        for source in range(devices)
    ]
    return [jnp.concatenate(ordered, axis=0), rest]


def per_device(samples, flags, delays, order):
    devices = lax.axis_size("chan")
    antennas_here, _, in_frames, chans = samples.shape
    local_channels = chans // devices
    spectra = in_frames - TAPS + 1
    antennas = antennas_here * devices
    beam_count = delays.shape[0]
    block = CHUNK_ANTENNAS if antennas_here > CHUNK_ANTENNAS else antennas_here
    paired = devices & (devices - 1) == 0 and antennas_here > block
    sizes = [block, antennas_here - block] if paired else [antennas_here]

    proto = jnp.asarray(prototype(TAPS, chans))
    table = jnp.asarray(transform_table(chans))

    me = lax.axis_index("chan")
    parts = []
    columns_of = []
    start = 0
    for size in sizes:
        pieces = devices if len(sizes) > 1 and start == 0 else 1
        parts.append(channelize(me, samples, proto, table, start, size, pieces))
        ids = np.arange(antennas, dtype=np.int32).reshape(devices, antennas_here)
        columns_of.append(ids[:, start : start + size].reshape(-1))
        start += size
    ids = np.concatenate(columns_of)
    if len(parts) > 1:
        parts = exchange_early(parts[0], parts[1][0])
    else:
        parts = [turn(parts[0][0])]
    blocks = [
        x.reshape(devices, local_channels, size, 2 * spectra) for x, size in zip(parts, sizes)
    ]

    def arrange(x):
        x = x.reshape(x.shape[:-1] + (devices, antennas_here))
        pieces = []
        at = 0
        for size in sizes:
            pieces.append(x[..., at : at + size].reshape(x.shape[:-2] + (devices * size,)))
            at += size
        return jnp.concatenate(pieces, axis=-1)

    flag_row = arrange(flags).astype(jnp.float32)
    keep = flag_row[None, :] * (1.0 / math.sqrt(antennas))
    weights = make_weights(
        arrange(delays), keep, lax.axis_index("chan") * local_channels, local_channels, chans
    )
    beams = form_beams(blocks, weights)
    arranged = turn(beams)
    arranged = arranged.reshape(devices, beam_count // devices, local_channels, 2 * spectra)
    visibilities = correlate(blocks, order, jnp.asarray(ids), flag_row)
    voltages = synthesize(arranged, proto, table)
    return visibilities, voltages


def solution(mesh):
    in_specs = (P(("groups", "chan"), None, None, None), P("groups"), P(), P("groups"))
    out_specs = (
        P(("groups", "chan"), None, None, None, None),
        P(("groups", "chan"), None, None, None),
    )

    return jax.shard_map(
        per_device, mesh=mesh, in_specs=in_specs, out_specs=out_specs, check_vma=False
    )
```
